32 devices in a mesh: groups: 2 (over y), gx: 16 (over z, x, core).
Axes of the slice: x: 2, y: 2, z: 4, core: 2. Of those that a mesh axis runs over, the one named last changes fastest.
Arguments:
- features: float32 [48, 64, 96, 128], P(None, ('groups', 'gx')), parts along dimension 1, may hold values from -6 to 6
- fine_weights: bfloat16 [1536, 8, 48, 48], P('gx'), may hold values from -1.796875 to 1.796875
- middle_weights: bfloat16 [384, 4, 48, 48], P('gx'), may hold values from -3 to 3
- lift_fine: float32 [48, 48], replicated, may hold values from -0.875 to 0.875
- lift_middle: float32 [48, 48], replicated, may hold values from -0.875 to 0.875
- project_out: float32 [48, 48], replicated, may hold values from -0.875 to 0.875
Outputs:
- result: float32 [48, 64, 96, 128], P(None, ('groups', 'gx')), parts along dimension 1
The draws below stay inside these ranges and needn't reach their ends.
There are 2 independent parts, one for each index of `groups`. The reference program is written for one: setup_inputs(seed, part) draws one part's arguments, and reference() takes and returns one part's arrays. A program takes and returns all parts, laid end to end along the dimension named above; an argument that names none is the same for every part. Nothing has to cross between parts.
All inputs are finite; a program needn't handle non-finite values.
Results may differ from the reference program's by a relative error of at most 0.0018.
Values sent between devices are 32-bit elements; how exact they have to be, the bound alone decides.
A program may use at most 128 MiB of HBM per device.

```python
import jax
import jax.numpy as jnp
from jax import lax

C = 48
NY = 96
NZ = 128
KY = 48
KZ = 32
NX = 32
KX = 8
KX2 = 4
MODES = 1536
MODES2 = 384


def levels(own_key, dims, split, smallest, top_value):
    loudness = 1.0
    for dim, parts in split:
        steps = jax.random.uniform(jax.random.fold_in(jax.random.fold_in(own_key, 6), dim), (parts,), jnp.float32, smallest / len(split), top_value / len(split))
        loudness = loudness * jnp.repeat(jnp.exp(steps), dims[dim] // parts).reshape((-1,) + (1,) * (len(dims) - 1 - dim))
    return loudness


def normal_values(own_key, dims, scale, limit, split=(), kind=jnp.bfloat16):
    drawn = scale * jax.random.normal(own_key, dims, jnp.float32)
    if split:
        drawn = drawn * levels(own_key, dims, split, -0.22, 0.18)
    return jnp.clip(drawn, -limit, limit).astype(kind)


def setup_inputs(seed: int = 0, part: int = 0) -> dict:
    streams_of = jax.random.split(jax.random.key(seed), 7)
    part_keys = jax.random.split(jax.random.fold_in(streams_of[6], part), 7)
    features = normal_values(part_keys[0], (C, NX, NY, NZ), 1.0, 6.0, ((1, 16),), jnp.float32)
    fine_weights = normal_values(streams_of[1], (MODES, KX, C, C), 0.3, 1.796875, ((0, 16),))
    middle_weights = normal_values(streams_of[2], (MODES2, KX2, C, C), 0.5, 3.0, ((0, 16),))
    lift_fine = normal_values(streams_of[3], (C, C), C ** -0.5, 0.875, (), jnp.float32)
    lift_middle = normal_values(streams_of[4], (C, C), C ** -0.5, 0.875, (), jnp.float32)
    project_out = normal_values(streams_of[5], (C, C), C ** -0.5, 0.875, (), jnp.float32)
    return dict(features=features, fine_weights=fine_weights, middle_weights=middle_weights, lift_fine=lift_fine, lift_middle=lift_middle, project_out=project_out)


HIGHEST = lax.Precision.HIGHEST

def cosine_table(modes_kept, length, offset, columns):
    orders = jnp.arange(modes_kept, dtype=jnp.int32)[:, None]
    points = offset + jnp.arange(columns, dtype=jnp.int32)[None, :]
    phase = orders * (2 * points + 1) % (4 * length)
    angle = jnp.pi / (2 * length) * phase.astype(jnp.float32)
    scales = jnp.where(orders == 0, jnp.sqrt(jnp.float32(1.0 / length)), jnp.sqrt(jnp.float32(2.0 / length)))
    return scales.astype(jnp.float32) * jnp.cos(angle)

def forward_yz(values, modes_y, modes_z):
    channels, local_x, cells_y, cells_z = values.shape
    table_z = cosine_table(modes_z, cells_z, 0, cells_z)
    table_y = cosine_table(modes_y, cells_y, 0, cells_y)
    along_z = jnp.einsum('cxyz,jz->cxyj', values, table_z, precision=HIGHEST)
    both = jnp.einsum('cxyj,iy->ijxc', along_z, table_y, precision=HIGHEST)
    return both.reshape(modes_y * modes_z, local_x, channels)

def inverse_yz(coeffs, modes_y, modes_z, cells_y, cells_z):
    total, local_x, channels = coeffs.shape
    shaped = coeffs.reshape(modes_y, modes_z, local_x, channels)
    table_z = cosine_table(modes_z, cells_z, 0, cells_z)
    table_y = cosine_table(modes_y, cells_y, 0, cells_y)
    along_y = jnp.einsum('ijxc,iy->jxcy', shaped, table_y, precision=HIGHEST)
    return jnp.einsum('jxcy,jz->cxyz', along_y, table_z, precision=HIGHEST)

def spectral(values, weights, modes_x, modes_y, modes_z):
    channels, cells_x, cells_y, cells_z = values.shape
    coeffs = forward_yz(values, modes_y, modes_z)
    table_x = cosine_table(modes_x, cells_x, 0, cells_x)
    modal = jnp.einsum('mxc,kx->mkc', coeffs, table_x, precision=HIGHEST)
    modal_b = modal.astype(jnp.bfloat16)
    mixed = jnp.einsum('mkc,mkco->mko', modal_b.astype(jnp.float32), weights.astype(jnp.float32), precision=HIGHEST)
    back = jnp.einsum('mkc,kx->mxc', mixed, table_x, precision=HIGHEST)
    return inverse_yz(back, modes_y, modes_z, cells_y, cells_z)

def pointwise(values, matrix):
    return jnp.einsum('cxyz,co->oxyz', values, matrix, precision=HIGHEST)

def coarsen(values):
    channels, cells_x, cells_y, cells_z = values.shape
    shaped = values.reshape(channels, cells_x // 2, 2, cells_y // 2, 2, cells_z // 2, 2)
    return lax.optimization_barrier(jnp.mean(shaped, axis=(2, 4, 6)))

def refine(values):
    return jnp.repeat(jnp.repeat(jnp.repeat(values, 2, axis=1), 2, axis=2), 2, axis=3)

def reference(features, fine_weights, middle_weights, lift_fine, lift_middle, project_out):
    level_one = jax.nn.gelu(spectral(features, fine_weights, KX, KY, KZ) + pointwise(features, lift_fine), approximate=False)
    pooled = coarsen(level_one)
    level_two = jax.nn.gelu(spectral(pooled, middle_weights, KX2, KY // 2, KZ // 2) + pointwise(pooled, lift_middle), approximate=False)
    return features + pointwise(level_one + refine(level_two), project_out)
```

```python
import functools

import jax
import jax.numpy as jnp
import numpy as np
from jax import lax
from jax.experimental import pallas as pl
from jax.experimental.pallas import tpu as pltpu
from jax.sharding import PartitionSpec as P

KY = 48
KZ = 32


HIGHEST = lax.Precision.HIGHEST


def cosine_table(modes_kept, length, columns):
    orders = jnp.arange(modes_kept, dtype=jnp.int32)[:, None]
    points = jnp.arange(columns, dtype=jnp.int32)[None, :]
    phase = orders * (2 * points + 1) % (4 * length)
    angle = jnp.pi / (2 * length) * phase.astype(jnp.float32)
    scales = jnp.where(
        orders == 0, jnp.sqrt(jnp.float32(1.0 / length)), jnp.sqrt(jnp.float32(2.0 / length))
    )
    return scales * jnp.cos(angle)


def forward_yz(values, modes_y, modes_z):
    channels, local_x, cells_y, cells_z = values.shape
    table_z = cosine_table(modes_z, cells_z, cells_z)
    table_y = cosine_table(modes_y, cells_y, cells_y)
    along_z = jnp.einsum("cxyz,jz->cxyj", values, table_z, precision=HIGHEST)
    both = jnp.einsum("cxyj,iy->ijxc", along_z, table_y, precision=HIGHEST)
    return both.reshape(modes_y * modes_z, local_x, channels)


def inverse_yz(coeffs, modes_y, modes_z, cells_y, cells_z):
    total, local_x, channels = coeffs.shape
    shaped = coeffs.reshape(modes_y, modes_z, local_x, channels)
    table_z = cosine_table(modes_z, cells_z, cells_z)
    table_y = cosine_table(modes_y, cells_y, cells_y)
    along_y = jnp.einsum("ijxc,iy->jxcy", shaped, table_y, precision=HIGHEST)
    return jnp.einsum("jxcy,jz->cxyz", along_y, table_z, precision=HIGHEST)


def mix_modes(modal, weights):
    return jnp.einsum(
        "mkc,mkco->mko", modal.astype(jnp.bfloat16), weights, preferred_element_type=jnp.float32
    )


def pointwise(values, matrix):
    return jnp.einsum("cxyz,co->oxyz", values, matrix, precision=HIGHEST)


def coarsen(values):
    channels, cells_x, cells_y, cells_z = values.shape
    shaped = values.reshape(channels, cells_x // 2, 2, cells_y // 2, 2, cells_z // 2, 2)
    return jnp.mean(shaped, axis=(2, 4, 6))


def refine(values):
    return jnp.repeat(jnp.repeat(jnp.repeat(values, 2, axis=1), 2, axis=2), 2, axis=3)


def general_device(features, fine_weights, middle_weights, lift_fine, lift_middle, project_out):
    channels, local_x, cells_y, cells_z = features.shape
    group_size = lax.axis_size("gx")
    cells_x = local_x * group_size
    modes_x = fine_weights.shape[1]
    coeffs = forward_yz(features, KY, KZ)
    table_x = cosine_table(modes_x, cells_x, cells_x)
    owned_pairs = coeffs.shape[0] // group_size
    grouped = coeffs.reshape(group_size, owned_pairs, local_x, channels)
    modal = jnp.einsum(
        "amxc,kx->mkc",
        lax.all_to_all(grouped, "gx", split_axis=0, concat_axis=2, tiled=True),
        table_x,
        precision=HIGHEST,
    )
    mixed = mix_modes(modal, fine_weights)
    back = jnp.einsum("mkc,kx->mxc", mixed, table_x, precision=HIGHEST)
    slabs = lax.all_to_all(back, "gx", split_axis=1, concat_axis=0, tiled=True)
    level_one = jax.nn.gelu(
        inverse_yz(slabs, KY, KZ, cells_y, cells_z) + pointwise(features, lift_fine),
        approximate=False,
    )
    pooled = coarsen(level_one)
    half_x = local_x // 2
    half_ky = KY // 2
    half_kz = KZ // 2
    half_modes = middle_weights.shape[1]
    coarse_x = half_x * group_size
    coarse_coeffs = forward_yz(pooled, half_ky, half_kz)
    coarse_pencils = lax.all_to_all(coarse_coeffs, "gx", split_axis=0, concat_axis=1, tiled=True)
    coarse_table = cosine_table(half_modes, coarse_x, coarse_x)
    coarse_modal = jnp.einsum("mxc,kx->mkc", coarse_pencils, coarse_table, precision=HIGHEST)
    coarse_mixed = mix_modes(coarse_modal, middle_weights)
    coarse_back = jnp.einsum("mkc,kx->mxc", coarse_mixed, coarse_table, precision=HIGHEST)
    coarse_slabs = lax.all_to_all(coarse_back, "gx", split_axis=1, concat_axis=0, tiled=True)
    level_two = jax.nn.gelu(
        inverse_yz(coarse_slabs, half_ky, half_kz, cells_y // 2, cells_z // 2)
        + pointwise(pooled, lift_middle),
        approximate=False,
    )
    return features + pointwise(level_one + refine(level_two), project_out)


BF16 = jnp.bfloat16
MESH = pl.DeviceIdType.MESH
F32 = jnp.float32


def host_table(modes_kept, length):
    orders = np.arange(modes_kept)[:, None]
    points = np.arange(length)[None, :]
    scales = np.where(orders == 0, np.sqrt(1.0 / length), np.sqrt(2.0 / length))
    return scales * np.cos(np.pi * orders * (2 * points + 1) / (2 * length))


def host_split(table):
    table = np.asarray(table, np.float32)
    high = table.astype(jnp.bfloat16)
    low = (table - high.astype(np.float32)).astype(jnp.bfloat16)
    return high, low


def left_rows(table):
    high, low = host_split(table)
    return jnp.asarray(
        np.concatenate([np.concatenate([high, high], 1), np.concatenate([low, low], 1)], 0)
    )


def left_three(table):
    high, low = host_split(table)
    return jnp.asarray(np.concatenate([high, high, low], 1))


def right_three(table):
    high, low = host_split(table)
    return jnp.asarray(np.concatenate([high, high, low], 0))


def split(values):
    high = values.astype(BF16)
    low = (values - high.astype(F32)).astype(BF16)
    return high, low


def dot(left, right):
    return jnp.dot(left, right, preferred_element_type=F32)


def dot_left3(left3, values):
    high, low = split(values)
    return dot(left3, jnp.concatenate([high, low, high], 0))


def dot_right3(values, right3):
    high, low = split(values)
    return dot(jnp.concatenate([high, low, high], 1), right3)


def gelu(t):
    return 0.5 * t * (1.0 + lax.erf(t * np.float32(np.sqrt(0.5))))


def far():
    return pl.BlockSpec(memory_space=pl.ANY)


def whole():
    return pl.BlockSpec(memory_space=pltpu.VMEM)


def widen(matrix_ref, targets):
    channels = matrix_ref.shape[0]
    size = channels * 8
    row = lax.broadcasted_iota(jnp.int32, (size, channels), 0) // 8
    pick = (row == lax.broadcasted_iota(jnp.int32, (size, channels), 1)).astype(F32).astype(BF16)
    col = lax.broadcasted_iota(jnp.int32, (channels, size), 1) // 8
    place = (col == lax.broadcasted_iota(jnp.int32, (channels, size), 0)).astype(F32).astype(BF16)
    left = lax.broadcasted_iota(jnp.int32, (size, size), 0) % 8
    right = lax.broadcasted_iota(jnp.int32, (size, size), 1) % 8
    for part, spots in zip(split(matrix_ref[...]), ((0, 1), (2,))):
        grown = lax.dot_general(pick, part, (((1,), (1,)), ((), ())), preferred_element_type=F32)
        grown = dot(grown.astype(BF16), place)
        for ref, at, rule in targets:
            value = jnp.where(rule(left, right), grown, 0.0).astype(BF16)
            for spot in spots:
                ref[at : at + size, spot * size : (spot + 1) * size] = value


def same(left, right):
    return left == right


def load_block(ref, at):
    channels, local_x, _, cells_z = ref.shape
    return jnp.concatenate([ref[:, x, at, :].reshape(channels * 8, cells_z) for x in range(local_x)], 1)


def store_block(ref, at, value):
    channels, local_x, _, cells_z = ref.shape
    for x in range(local_x):
        ref[:, x, at, :] = value[:, x * cells_z : (x + 1) * cells_z].reshape(channels, 8, cells_z)


def greet(n):
    me = lax.axis_index("gx")
    barrier = pltpu.get_barrier_semaphore()
    for d in range(1, n):
        pl.semaphore_signal(barrier, 1, device_id={"gx": lax.rem(me + d, n)}, device_id_type=MESH)
    pl.semaphore_wait(barrier, n - 1)


class Exchange:
    def __init__(self, n, source, target, send_sem, recv_sem, own_sem):
        self.n, self.source, self.target = n, source, target
        self.send_sem, self.recv_sem, self.own_sem = send_sem, recv_sem, own_sem
        self.me = lax.axis_index("gx")

    def copy(self, slot, d):
        peer = lax.rem(self.me + d, self.n)
        return pltpu.make_async_remote_copy(
            src_ref=self.source.at[slot, peer],
            dst_ref=self.target.at[slot, self.me],
            send_sem=self.send_sem.at[slot, d],
            recv_sem=self.recv_sem.at[slot, d],
            device_id={"gx": peer},
            device_id_type=MESH,
        )

    def own(self, slot):
        return pltpu.make_async_copy(
            self.source.at[slot, self.me], self.target.at[slot, self.me], self.own_sem.at[slot]
        )

    def start(self, slot):
        def send(d, carry):
            self.copy(slot, d).start()
            return carry

        lax.fori_loop(1, self.n, send, 0, unroll=True)
        self.own(slot).start()

    def wait(self, slot):
        def one(d, carry):
            self.copy(slot, d).wait()
            return carry

        lax.fori_loop(1, self.n, one, 0, unroll=True)
        self.own(slot).wait()


CHUNK = 16
TABLES = 8


def main_kernel(n, tx, txc, *refs):
    refs = list(refs)
    f_hbm, w_hbm, wm_hbm, lift_ref, middle_ref, project_ref = refs[:6]
    table_hbm = refs[6 : 6 + TABLES]
    slab_ref, lifted_ref, base_hbm, final_wide = refs[6 + TABLES : 10 + TABLES]
    rest = refs[10 + TABLES :]
    tables = rest[:TABLES]
    (
        f_ref, w_ref, wm_ref, lev_ref, grown_ref, wire_one, got_one, wire_two, got_two,
        modal, mixed, sum_ref, pooled_ref, coarse_ref, stage, got_three, back_c, got_four,
        lift_wide, middle_wide, proj_wide,
        send_one, recv_one, own_one, send_two, recv_two, own_two,
        send_three, recv_three, own_three, send_four, recv_four, own_four,
        f_sem, w_sem, wm_sem, table_sem, save_sem,
    ) = rest[TABLES:]
    ty_ref, tz_ref, tyi_ref, tzi_ref, yc_ref, zc_ref, zp_ref, perm_ref = tables
    channels, local_x, cells_y, cells_z = f_ref.shape
    modes_x, _, _, owned = w_ref.shape
    modes_y = ty_ref.shape[0] // 2
    per = modes_y // n
    chunks = channels // CHUNK
    rows = local_x * CHUNK
    half = CHUNK // 2
    quad = 4

    loads = [
        pltpu.make_async_copy(
            f_hbm.at[pl.ds(q * CHUNK, CHUNK)], f_ref.at[pl.ds(q * CHUNK, CHUNK)], f_sem.at[q]
        )
        for q in range(chunks)
    ]
    fills = [
        pltpu.make_async_copy(source, target, table_sem.at[i])
        for i, (source, target) in enumerate(zip(table_hbm, tables))
    ]
    loads[0].start()
    fills[0].start()
    fills[1].start()
    for load in loads[1:]:
        load.start()
    for fill in fills[2:]:
        fill.start()
    fetch = pltpu.make_async_copy(w_hbm, w_ref, w_sem)
    fetch.start()
    fetch_c = pltpu.make_async_copy(wm_hbm, wm_ref, wm_sem)
    fetch_c.start()

    me = lax.axis_index("gx")
    barrier = pltpu.get_barrier_semaphore()
    for d in range(1, n):
        pl.semaphore_signal(barrier, 1, device_id={"gx": lax.rem(me + d, n)}, device_id_type=MESH)

    one = Exchange(n, wire_one, got_one, send_one, recv_one, own_one)
    two = Exchange(n, wire_two, got_two, send_two, recv_two, own_two)
    three = Exchange(n, stage, got_three, send_three, recv_three, own_three)
    four = Exchange(n, back_c, got_four, send_four, recv_four, own_four)

    fills[0].wait()
    fills[1].wait()
    tail_lane = lax.broadcasted_iota(jnp.int32, (3 * half, 128), 1) // 32

    def forward(q, carry):
        pltpu.make_async_copy(
            f_hbm.at[pl.ds(q * CHUNK, CHUNK)], f_ref.at[pl.ds(q * CHUNK, CHUNK)], f_sem.at[q]
        ).wait()

        def channel(c, inner):
            wide = jnp.concatenate([f_ref[q * CHUNK + c, x] for x in range(local_x)], 1)
            high, low = split(wide)
            both = dot(ty_ref[...], jnp.concatenate([high, low], 0))
            both = both[:modes_y] + both[modes_y:]
            for x in range(local_x):
                grown_ref[pl.ds(x * CHUNK + c, modes_y, stride=rows), :] = both[
                    :, x * cells_z : (x + 1) * cells_z
                ]
            return inner

        lax.fori_loop(0, CHUNK, channel, 0, unroll=8)

        def owners(b, inner):
            size = quad * per * rows
            done = dot_right3(grown_ref[pl.ds(pl.multiple_of(b * size, 8), size), :], tz_ref[...])
            for k in range(quad):
                part = done[k * per * rows : (k + 1) * per * rows]
                total = jnp.concatenate(
                    [part[g * rows + 3 * half : (g + 1) * rows] for g in range(per)], 0
                )
                for g in range(per):
                    total = jnp.where(tail_lane == g, part[g * rows : g * rows + 3 * half], total)
                wire_one[q, b * quad + k] = total
            return inner

        lax.fori_loop(0, n // quad, owners, 0, unroll=2)

        @pl.when(q == 0)
        def _():
            pl.semaphore_wait(barrier, n - 1)

        one.start(q)
        return carry

    lax.fori_loop(0, chunks, forward, 0)

    widen(lift_ref, ((lift_wide, 0, same),))

    def lift(b, carry):
        at = pl.ds(pl.multiple_of(b * 8, 8), 8)
        store_block(lev_ref, at, dot_left3(lift_wide[...], load_block(f_ref, at)))
        return carry

    lax.fori_loop(0, cells_y // 8, lift, 0)
    mixed[...] = jnp.zeros_like(mixed)
    for fill in fills[2:]:
        fill.wait()
    fetch.wait()
    fetch_c.wait()

    small_lane = lax.broadcasted_iota(jnp.int32, (half, 128), 1) // 32

    def absorb(q, carry):
        one.wait(q)
        for k in range(modes_x):
            first = sum(got_one[q, a, :CHUNK] * np.float32(tx[k, a, 0]) for a in range(n))
            second = sum(got_one[q, a] * np.float32(tx[k, a, 1]) for a in range(n))
            extra = jnp.zeros((half, 128), F32)
            for g in range(3):
                piece = pltpu.roll(second[g * half : (g + 1) * half], 32 * (g + 1), 1)
                extra = jnp.where(small_lane == g, piece, extra)
            total = first + jnp.concatenate([second[CHUNK:], extra], 0)
            modal[k, pl.ds(pl.multiple_of(q * CHUNK, 8), CHUNK)] = total.astype(BF16).astype(F32)

        @pl.when(q < chunks - 1)
        def _():
            def mode(k, inner):
                total = mixed[k, :, :owned]
                for c in range(CHUNK):
                    at = q * CHUNK + c
                    total += modal[k, pl.ds(at, 1), :owned] * w_ref[k, at].astype(F32)
                mixed[k, :, :owned] = total
                return inner

            lax.fori_loop(0, modes_x, mode, 0, unroll=2)

        return carry

    lax.fori_loop(0, chunks, absorb, 0)

    wide_lane = lax.broadcasted_iota(jnp.int32, (3 * half, 128), 1)

    def back(h, carry):
        at = pl.ds(pl.multiple_of(h * CHUNK, CHUNK), CHUNK)

        def mode(k, inner):
            total = mixed[k, at, :owned]
            for c in range(channels - CHUNK, channels):
                total += modal[k, c : c + 1, :owned] * w_ref[k, c, at].astype(F32)
            mixed[k, at, :owned] = total
            return inner

        lax.fori_loop(0, modes_x, mode, 0, unroll=2)
        value = [mixed[k, at] for k in range(modes_x)]
        for a in range(n):
            first = sum(value[k] * np.float32(tx[k, a, 0]) for k in range(modes_x))
            second = sum(value[k] * np.float32(tx[k, a, 1]) for k in range(modes_x))
            rolled = jnp.concatenate(
                [pltpu.roll(second[half:], 96 - 32 * g, 1) for g in range(3)], 0
            )
            wire_two[h, a] = jnp.where(
                wide_lane < 96, jnp.concatenate([first, second[:half]], 0), rolled
            )
        two.start(h)
        return carry

    lax.fori_loop(0, chunks, back, 0)

    size = channels * 8
    widen(middle_ref, ((middle_wide, 0, same),))
    widen(
        project_ref,
        (
            (proj_wide, 0, same),
            (final_wide, 0, lambda left, right: left // 2 == right),
            (final_wide, size, lambda left, right: left // 2 + 4 == right),
        ),
    )

    lane = lax.broadcasted_iota(jnp.int32, (rows, 128), 1) // 32
    tail = lax.broadcasted_iota(jnp.int32, (rows, 128), 0) >= 3 * half
    half_y = cells_y // 2
    modes_c = yc_ref.shape[0] // 2 - half_y
    parts = zc_ref.shape[1] // 128
    narrow = 128 // CHUNK
    coarse_lane = (
        lax.broadcasted_iota(jnp.int32, (modes_c, parts * 128), 1) // narrow % CHUNK
    )
    c_rows = modes_c + half_y

    def middle(h, carry):
        two.wait(h)

        def inverse(b, inner):
            lefts = []
            for k in range(quad):
                a = b * quad + k
                for g in range(per):
                    value = jnp.concatenate(
                        [got_two[h, a], got_two[h, a, g * half : (g + 1) * half]], 0
                    )
                    lefts.append(jnp.where(lane == jnp.where(tail, 3, g), value, 0.0))
            done = dot_right3(jnp.concatenate(lefts, 0), tzi_ref[...])
            size = quad * per * rows
            grown_ref[pl.ds(pl.multiple_of(b * size, 8), size), :] = done
            return inner

        lax.fori_loop(0, n // quad, inverse, 0, unroll=2)

        def level(o, inner):
            wide = jnp.concatenate(
                [grown_ref[pl.ds(x * CHUNK + o, modes_y, stride=rows), :] for x in range(local_x)], 1
            )
            done = dot_left3(tyi_ref[...], wide)
            at = h * CHUNK + o
            values = []
            for x in range(local_x):
                value = gelu(lev_ref[at, x] + done[:, x * cells_z : (x + 1) * cells_z])
                lev_ref[at, x] = value
                values.append(value)
            sum_ref[o] = values[0] + values[1]
            return inner

        lax.fori_loop(0, CHUNK, level, 0, unroll=4)

        total = jnp.zeros((modes_c, parts * 128), F32)
        for pair in range(CHUNK // 2):
            wide = jnp.concatenate([sum_ref[2 * pair], sum_ref[2 * pair + 1]], 1)
            high, low = split(wide)
            both = dot(yc_ref[...], jnp.concatenate([high, low], 0))
            both = both[:c_rows] + both[c_rows:]
            modes = jnp.concatenate([both[half_y:, :128], both[half_y:, 128:]], 0)
            done = dot_right3(modes, zc_ref[...])
            for k in range(2):
                total = jnp.where(
                    coarse_lane == pair * 2 + k, done[k * modes_c : (k + 1) * modes_c], total
                )
            flat = jnp.concatenate([both[:half_y, :128], both[:half_y, 128:]], 0)
            high, low = split(flat)
            mean = dot(jnp.concatenate([high, low], 1), zp_ref[...])
            pooled_ref[h * CHUNK + 2 * pair] = mean[:half_y]
            pooled_ref[h * CHUNK + 2 * pair + 1] = mean[half_y:]
        for p in range(parts):
            coarse_ref[pl.ds(h * modes_c * parts + p, modes_c, stride=parts), :] = total[
                :, p * 128 : (p + 1) * 128
            ]
        return carry

    lax.fori_loop(0, chunks, middle, 0)

    count = stage.shape[2]
    c_size = modes_c * parts
    for a in range(n):
        for h in range(chunks):
            stage[0, a, :, h * 128 : (h + 1) * 128] = coarse_ref[
                h * c_size + a * count : h * c_size + (a + 1) * count
            ]
    three.start(0)

    def project(b, carry):
        at = pl.ds(pl.multiple_of(b * 8, 8), 8)
        done = dot_left3(proj_wide[...], load_block(lev_ref, at))
        store_block(f_ref, at, load_block(f_ref, at) + done)
        return carry

    blocks = cells_y // 8
    cut = blocks // 2 * 8
    lax.fori_loop(0, blocks // 2, project, 0, unroll=3)
    low_save = pltpu.make_async_copy(
        f_ref.at[:, :, pl.ds(0, cut), :], base_hbm.at[:, :, pl.ds(0, cut), :], save_sem.at[0]
    )
    low_save.start()

    three.wait(0)
    modes_k = wm_ref.shape[1]
    wave = [
        sum(got_three[0, a] * np.float32(txc[k, a]) for a in range(n)) for k in range(modes_k)
    ]
    wave = jnp.concatenate(wave, 0).astype(BF16)
    turned = dot(wave, perm_ref[:, : wave.shape[1]])
    width = wave.shape[1]
    keep = (
        lax.broadcasted_iota(jnp.int32, (narrow, width), 1) // channels
        == lax.broadcasted_iota(jnp.int32, (narrow, width), 0)
    )
    outs = []
    for k in range(modes_k):
        for t in range(count):
            row = turned[k * count + t : k * count + t + 1]
            left = jnp.where(keep, jnp.broadcast_to(row, (narrow, width)), 0.0).astype(BF16)
            right = wm_ref[t * narrow : (t + 1) * narrow, k].reshape(narrow * channels, channels)
            outs.append(dot(left, right))
    high, low = split(jnp.concatenate(outs, 0))
    spread = perm_ref[: 2 * channels, width:]
    grown = dot(jnp.concatenate([high, low], 1), spread)
    ours = (
        lax.broadcasted_iota(jnp.int32, grown.shape, 1) % narrow
        == lax.broadcasted_iota(jnp.int32, grown.shape, 0) % narrow
    )
    grown = jnp.where(ours, grown, 0.0).reshape(modes_k * count, narrow, width).sum(1)
    for a in range(n):
        back_c[0, a] = sum(
            grown[k * count : (k + 1) * count] * np.float32(txc[k, a]) for k in range(modes_k)
        )
    four.start(0)

    def lift_coarse(g, carry):
        at = [pl.ds(pl.multiple_of(g * 16 + 8 * k, 8), 8) for k in range(2)]
        pooled = jnp.concatenate([pooled_ref[:, a, :].reshape(channels * 8, 128) for a in at], 1)
        done = dot_left3(middle_wide[...], pooled)
        for k in range(2):
            lifted_ref[:, at[k], :] = done[:, k * 128 : (k + 1) * 128].reshape(channels, 8, 128)
        return carry

    lax.fori_loop(0, half_y // 16, lift_coarse, 0)
    lax.fori_loop(blocks // 2, blocks, project, 0, unroll=3)
    high_save = pltpu.make_async_copy(
        f_ref.at[:, :, pl.ds(cut, cells_y - cut), :],
        base_hbm.at[:, :, pl.ds(cut, cells_y - cut), :],
        save_sem.at[1],
    )
    high_save.start()
    four.wait(0)
    for a in range(n):
        for h in range(chunks):
            slab_ref[h * c_size + a * count : h * c_size + (a + 1) * count, :] = got_four[
                0, a, :, h * 128 : (h + 1) * 128
            ]
    low_save.wait()
    high_save.wait()


def main_call(n, tx, txc, features, weights, middle_weights, matrices, tables):
    channels, local_x, cells_y, cells_z = features.shape
    turned = jnp.transpose(weights, (1, 2, 3, 0))
    modes_x = turned.shape[0]
    size = channels * 8
    chunks = channels // CHUNK
    wire = (chunks, n, 3 * CHUNK // 2, 128)
    c_rows = (KY // 2) * (KZ // 2) // (128 // CHUNK)
    coarse = (1, n, c_rows // n, channels * 128 // CHUNK)
    wide = (size, 3 * size)

    def sems(slots):
        return [
            pltpu.SemaphoreType.DMA((slots, n)),
            pltpu.SemaphoreType.DMA((slots, n)),
            pltpu.SemaphoreType.DMA((slots,)),
        ]

    return pl.pallas_call(
        functools.partial(main_kernel, n, tx, txc),
        out_shape=(
            jax.ShapeDtypeStruct((c_rows * chunks, 128), F32),
            jax.ShapeDtypeStruct((channels, cells_y // 2, 128), F32),
            jax.ShapeDtypeStruct(features.shape, F32),
            jax.ShapeDtypeStruct((2 * size, 3 * size), BF16),
        ),
        in_specs=[far()] * 3 + [whole()] * 3 + [far()] * TABLES,
        out_specs=(whole(), whole(), far(), whole()),
        scratch_shapes=[pltpu.VMEM(table.shape, table.dtype) for table in tables]
        + [
            pltpu.VMEM(features.shape, F32),
            pltpu.VMEM(turned.shape, BF16),
            pltpu.VMEM(middle_weights.shape, BF16),
            pltpu.VMEM(features.shape, F32),
            pltpu.VMEM((KY * local_x * CHUNK, cells_z), F32),
            pltpu.VMEM(wire, F32),
            pltpu.VMEM(wire, F32),
            pltpu.VMEM(wire, F32),
            pltpu.VMEM(wire, F32),
            pltpu.VMEM((modes_x, channels, 128), F32),
            pltpu.VMEM((modes_x, channels, 128), F32),
            pltpu.VMEM((CHUNK, cells_y, cells_z), F32),
            pltpu.VMEM((channels, cells_y // 2, 128), F32),
            pltpu.VMEM((c_rows * chunks, 128), F32),
            pltpu.VMEM(coarse, F32),
            pltpu.VMEM(coarse, F32),
            pltpu.VMEM(coarse, F32),
            pltpu.VMEM(coarse, F32),
            pltpu.VMEM(wide, BF16),
            pltpu.VMEM(wide, BF16),
            pltpu.VMEM(wide, BF16),
        ]
        + sems(chunks)
        + sems(chunks)
        + sems(1)
        + sems(1)
        + [
            pltpu.SemaphoreType.DMA((chunks,)),
            pltpu.SemaphoreType.DMA,
            pltpu.SemaphoreType.DMA,
            pltpu.SemaphoreType.DMA((TABLES,)),
            pltpu.SemaphoreType.DMA((2,)),
        ],
        compiler_params=pltpu.CompilerParams(
            collective_id=0, has_side_effects=True, vmem_limit_bytes=60 * 1024 * 1024
        ),
        name="main",
    )(features, turned, middle_weights, *matrices, *tables)


def final_kernel(
    slab_hbm, ty_hbm, tz_hbm, lifted_hbm, proj_hbm, base_hbm, out_hbm,
    slab_ref, ty_ref, tz_ref, lifted_ref, proj_ref, base_ref, spec_ref, load_sem, save_sem,
):
    loads = [
        pltpu.make_async_copy(source, target, load_sem.at[i])
        for i, (source, target) in enumerate(
            (
                (slab_hbm, slab_ref), (ty_hbm, ty_ref), (tz_hbm, tz_ref),
                (lifted_hbm, lifted_ref), (proj_hbm, proj_ref), (base_hbm, base_ref),
            )
        )
    ]
    for load in loads:
        load.start()
    for load in loads[:3]:
        load.wait()
    channels, half_y, _ = lifted_ref.shape
    local_x = base_ref.shape[1]
    modes = ty_ref.shape[1] // 3
    parts = tz_ref.shape[0] // (3 * 128)
    chunks = channels // CHUNK
    c_size = modes * parts
    stacked = []
    for h in range(chunks):
        wide = jnp.concatenate(
            [slab_ref[pl.ds(h * c_size + p, modes, stride=parts), :] for p in range(parts)], 1
        )
        stacked.append(dot_left3(ty_ref[...], wide))
    grown = jnp.concatenate(stacked, 0)
    high, low = split(grown)
    left = jnp.concatenate([high, low, high], 1)
    lane = lax.broadcasted_iota(jnp.int32, left.shape, 1) // (128 // CHUNK) % CHUNK

    for c in range(CHUNK):
        done = dot(jnp.where(lane == c, left, jnp.zeros_like(left)), tz_ref[...])
        for h in range(chunks):
            spec_ref[h * CHUNK + c] = done[h * half_y : (h + 1) * half_y]

    for load in loads[3:]:
        load.wait()
    saves = []
    for g in range(half_y // 16):
        at = [pl.ds(g * 16 + 8 * k, 8) for k in range(2)]
        pooled = jnp.concatenate([lifted_ref[:, a, :].reshape(channels * 8, 128) for a in at], 1)
        spectral = jnp.concatenate([spec_ref[:, a, :].reshape(channels * 8, 128) for a in at], 1)
        added = dot_left3(proj_ref[...], gelu(pooled + spectral))
        for k in range(2):
            for b in range(2):
                piece = added[b * channels * 8 : (b + 1) * channels * 8, k * 128 : (k + 1) * 128]
                piece = piece.reshape(channels, 8, 128)
                rows = pl.ds(g * 32 + 16 * k + 8 * b, 8)
                for x in range(local_x):
                    base_ref[:, x, rows, :] += piece
        rows = pl.ds(g * 32, 32)
        save = pltpu.make_async_copy(
            base_ref.at[:, :, rows, :], out_hbm.at[:, :, rows, :], save_sem.at[g]
        )
        save.start()
        saves.append(save)
    for save in saves:
        save.wait()


def on_device(features, fine_weights, middle_weights, lift_fine, lift_middle, project_out):
    channels, local_x, cells_y, cells_z = features.shape
    n = lax.axis_size("gx")
    owned = fine_weights.shape[0]
    owned_c = middle_weights.shape[0]
    half_ky, half_kz = KY // 2, KZ // 2
    narrow = 128 // CHUNK
    fits = (
        owned == 3 * KZ
        and KZ == 32
        and KY == 3 * n
        and n % 4 == 0
        and owned_c % narrow == 0
        and local_x == 2
        and cells_z == 128
        and cells_y % 32 == 0
        and channels == 3 * CHUNK
    )
    if not fits:
        return general_device(
            features, fine_weights, middle_weights, lift_fine, lift_middle, project_out
        )
    modes_x = fine_weights.shape[1]
    modes_c = middle_weights.shape[1]
    tx = np.asarray(host_table(modes_x, local_x * n), np.float32).reshape(modes_x, n, local_x)
    txc = np.asarray(host_table(modes_c, n), np.float32)

    half_y, half_z = cells_y // 2, cells_z // 2
    pool_y = np.repeat(np.eye(half_y), 2, axis=1) * 0.5
    pool_z = np.repeat(np.eye(half_z), 2, axis=1) * 0.25
    ty_c = host_table(half_ky, half_y)
    tz_c = host_table(half_kz, half_z)
    parts = half_kz // narrow
    chunks = channels // CHUNK
    ty = left_rows(host_table(KY, cells_y))
    tz = right_three(np.tile(host_table(KZ, cells_z).T, (1, 4)))
    yc = left_rows(np.concatenate([pool_y, ty_c @ pool_y], 0))
    zc_full = (tz_c @ pool_z).T.reshape(cells_z, parts, 1, narrow)
    zc = right_three(np.broadcast_to(zc_full, (cells_z, parts, CHUNK, narrow)).reshape(cells_z, -1))
    zp = np.repeat(pool_z, 2, axis=0).T
    zp = np.asarray(zp, jnp.bfloat16)
    zp = jnp.asarray(np.concatenate([zp, zp], 0))
    ty_i = left_three(host_table(KY, cells_y).T)
    tz_i = right_three(np.tile(host_table(KZ, cells_z), (4, 1)))
    width = channels * narrow
    turn = np.zeros((width, 2 * width), np.float32)
    for c in range(channels):
        for j in range(narrow):
            turn[c * narrow + j, j * channels + c] = 1.0
            turn[c, width + c * narrow + j] = 1.0
            turn[channels + c, width + c * narrow + j] = 1.0
    turn = jnp.asarray(turn.astype(jnp.bfloat16))
    slab, lifted, base, projm = main_call(
        n, tx, txc, features, fine_weights, middle_weights,
        (lift_fine, lift_middle, project_out), (ty, tz, ty_i, tz_i, yc, zc, zp, turn),
    )

    tyc_i = left_three(ty_c.T)
    grown = np.repeat(tz_c, 2, axis=1).reshape(parts, 1, narrow, cells_z)
    tzc_i = right_three(np.broadcast_to(grown, (parts, CHUNK, narrow, cells_z)).reshape(-1, cells_z))
    return pl.pallas_call(
        final_kernel,
        out_shape=jax.ShapeDtypeStruct(features.shape, F32),
        in_specs=[far()] * 6,
        out_specs=far(),
        scratch_shapes=[
            pltpu.VMEM(value.shape, value.dtype)
            for value in (slab, tyc_i, tzc_i, lifted, projm, base)
        ]
        + [
            pltpu.VMEM((channels, half_y, 128), F32),
            pltpu.SemaphoreType.DMA((6,)),
            pltpu.SemaphoreType.DMA((half_y // 16,)),
        ],
        compiler_params=pltpu.CompilerParams(vmem_limit_bytes=60 * 1024 * 1024),
        name="final",
    )(slab, tyc_i, tzc_i, lifted, projm, base)


def solution(mesh):
    in_specs = (
        P(None, ("groups", "gx"), None, None),
        P("gx", None, None, None),
        P("gx", None, None, None),
        P(),
        P(),
        P(),
    )
    out_specs = P(None, ("groups", "gx"), None, None)
    return jax.shard_map(
        on_device, mesh=mesh, in_specs=in_specs, out_specs=out_specs, check_vma=False
    )
```

```python
import functools

import jax
import jax.numpy as jnp
import numpy as np
from jax import lax
from jax.experimental import pallas as pl
from jax.experimental.pallas import tpu as pltpu
from jax.sharding import PartitionSpec as P

KY = 48
KZ = 32


HIGHEST = lax.Precision.HIGHEST


def cosine_table(modes_kept, length, columns):
    orders = jnp.arange(modes_kept, dtype=jnp.int32)[:, None]
    points = jnp.arange(columns, dtype=jnp.int32)[None, :]
    phase = orders * (2 * points + 1) % (4 * length)
    angle = jnp.pi / (2 * length) * phase.astype(jnp.float32)
    scales = jnp.where(
        orders == 0, jnp.sqrt(jnp.float32(1.0 / length)), jnp.sqrt(jnp.float32(2.0 / length))
    )
    return scales * jnp.cos(angle)


def forward_yz(values, modes_y, modes_z):
    channels, local_x, cells_y, cells_z = values.shape
    table_z = cosine_table(modes_z, cells_z, cells_z)
    table_y = cosine_table(modes_y, cells_y, cells_y)
    along_z = jnp.einsum("cxyz,jz->cxyj", values, table_z, precision=HIGHEST)
    both = jnp.einsum("cxyj,iy->ijxc", along_z, table_y, precision=HIGHEST)
    return both.reshape(modes_y * modes_z, local_x, channels)


def inverse_yz(coeffs, modes_y, modes_z, cells_y, cells_z):
    total, local_x, channels = coeffs.shape
    shaped = coeffs.reshape(modes_y, modes_z, local_x, channels)
    table_z = cosine_table(modes_z, cells_z, cells_z)
    table_y = cosine_table(modes_y, cells_y, cells_y)
    along_y = jnp.einsum("ijxc,iy->jxcy", shaped, table_y, precision=HIGHEST)
    return jnp.einsum("jxcy,jz->cxyz", along_y, table_z, precision=HIGHEST)


def mix_modes(modal, weights):
    return jnp.einsum(
        "mkc,mkco->mko", modal.astype(jnp.bfloat16), weights, preferred_element_type=jnp.float32
    )


def pointwise(values, matrix):
    return jnp.einsum("cxyz,co->oxyz", values, matrix, precision=HIGHEST)


def coarsen(values):
    channels, cells_x, cells_y, cells_z = values.shape
    shaped = values.reshape(channels, cells_x // 2, 2, cells_y // 2, 2, cells_z // 2, 2)
    return jnp.mean(shaped, axis=(2, 4, 6))


def refine(values):
    return jnp.repeat(jnp.repeat(jnp.repeat(values, 2, axis=1), 2, axis=2), 2, axis=3)


def general_device(features, fine_weights, middle_weights, lift_fine, lift_middle, project_out):
    channels, local_x, cells_y, cells_z = features.shape
    group_size = lax.axis_size("gx")
    cells_x = local_x * group_size
    modes_x = fine_weights.shape[1]
    coeffs = forward_yz(features, KY, KZ)
    table_x = cosine_table(modes_x, cells_x, cells_x)
    owned_pairs = coeffs.shape[0] // group_size
    grouped = coeffs.reshape(group_size, owned_pairs, local_x, channels)
    modal = jnp.einsum(
        "amxc,kx->mkc",
        lax.all_to_all(grouped, "gx", split_axis=0, concat_axis=2, tiled=True),
        table_x,
        precision=HIGHEST,
    )
    mixed = mix_modes(modal, fine_weights)
    back = jnp.einsum("mkc,kx->mxc", mixed, table_x, precision=HIGHEST)
    slabs = lax.all_to_all(back, "gx", split_axis=1, concat_axis=0, tiled=True)
    level_one = jax.nn.gelu(
        inverse_yz(slabs, KY, KZ, cells_y, cells_z) + pointwise(features, lift_fine),
        approximate=False,
    )
    pooled = coarsen(level_one)
    half_x = local_x // 2
    half_ky = KY // 2
    half_kz = KZ // 2
    half_modes = middle_weights.shape[1]
    coarse_x = half_x * group_size
    coarse_coeffs = forward_yz(pooled, half_ky, half_kz)
    coarse_pencils = lax.all_to_all(coarse_coeffs, "gx", split_axis=0, concat_axis=1, tiled=True)
    coarse_table = cosine_table(half_modes, coarse_x, coarse_x)
    coarse_modal = jnp.einsum("mxc,kx->mkc", coarse_pencils, coarse_table, precision=HIGHEST)
    coarse_mixed = mix_modes(coarse_modal, middle_weights)
    coarse_back = jnp.einsum("mkc,kx->mxc", coarse_mixed, coarse_table, precision=HIGHEST)
    coarse_slabs = lax.all_to_all(coarse_back, "gx", split_axis=1, concat_axis=0, tiled=True)
    level_two = jax.nn.gelu(
        inverse_yz(coarse_slabs, half_ky, half_kz, cells_y // 2, cells_z // 2)
        + pointwise(pooled, lift_middle),
        approximate=False,
    )
    return features + pointwise(level_one + refine(level_two), project_out)


BF16 = jnp.bfloat16
MESH = pl.DeviceIdType.MESH
F32 = jnp.float32


def host_table(modes_kept, length):
    orders = np.arange(modes_kept)[:, None]
    points = np.arange(length)[None, :]
    scales = np.where(orders == 0, np.sqrt(1.0 / length), np.sqrt(2.0 / length))
    return scales * np.cos(np.pi * orders * (2 * points + 1) / (2 * length))


def host_split(table):
    table = np.asarray(table, np.float32)
    high = table.astype(jnp.bfloat16)
    low = (table - high.astype(np.float32)).astype(jnp.bfloat16)
    return high, low


def left_rows(table):
    high, low = host_split(table)
    return jnp.asarray(
        np.concatenate([np.concatenate([high, high], 1), np.concatenate([low, low], 1)], 0)
    )


def left_three(table):
    high, low = host_split(table)
    return jnp.asarray(np.concatenate([high, high, low], 1))


def right_three(table):
    high, low = host_split(table)
    return jnp.asarray(np.concatenate([high, high, low], 0))


def split(values):
    high = values.astype(BF16)
    low = (values - high.astype(F32)).astype(BF16)
    return high, low


def dot(left, right):
    return jnp.dot(left, right, preferred_element_type=F32)


def dot_left3(left3, values):
    high, low = split(values)
    return dot(left3, jnp.concatenate([high, low, high], 0))


def dot_right3(values, right3):
    high, low = split(values)
    return dot(jnp.concatenate([high, low, high], 1), right3)


def gelu(t):
    return 0.5 * t * (1.0 + lax.erf(t * np.float32(np.sqrt(0.5))))


def far():
    return pl.BlockSpec(memory_space=pl.ANY)


def whole():
    return pl.BlockSpec(memory_space=pltpu.VMEM)


def widen(matrix_ref, targets):
    channels = matrix_ref.shape[0]
    size = channels * 8
    row = lax.broadcasted_iota(jnp.int32, (size, channels), 0) // 8
    pick = (row == lax.broadcasted_iota(jnp.int32, (size, channels), 1)).astype(F32).astype(BF16)
    col = lax.broadcasted_iota(jnp.int32, (channels, size), 1) // 8
    place = (col == lax.broadcasted_iota(jnp.int32, (channels, size), 0)).astype(F32).astype(BF16)
    left = lax.broadcasted_iota(jnp.int32, (size, size), 0) % 8
    right = lax.broadcasted_iota(jnp.int32, (size, size), 1) % 8
    for part, spots in zip(split(matrix_ref[...]), ((0, 1), (2,))):
        grown = lax.dot_general(pick, part, (((1,), (1,)), ((), ())), preferred_element_type=F32)
        grown = dot(grown.astype(BF16), place)
        for ref, at, rule in targets:
            value = jnp.where(rule(left, right), grown, 0.0).astype(BF16)
            for spot in spots:
                ref[at : at + size, spot * size : (spot + 1) * size] = value


def same(left, right):
    return left == right


def load_block(ref, at):
    channels, local_x, _, cells_z = ref.shape
    return jnp.concatenate([ref[:, x, at, :].reshape(channels * 8, cells_z) for x in range(local_x)], 1)


def store_block(ref, at, value):
    channels, local_x, _, cells_z = ref.shape
    for x in range(local_x):
        ref[:, x, at, :] = value[:, x * cells_z : (x + 1) * cells_z].reshape(channels, 8, cells_z)


def greet(n):
    me = lax.axis_index("gx")
    barrier = pltpu.get_barrier_semaphore()
    for d in range(1, n):
        pl.semaphore_signal(barrier, 1, device_id={"gx": lax.rem(me + d, n)}, device_id_type=MESH)
    pl.semaphore_wait(barrier, n - 1)


class Exchange:
    def __init__(self, n, source, target, send_sem, recv_sem, own_sem):
        self.n, self.source, self.target = n, source, target
        self.send_sem, self.recv_sem, self.own_sem = send_sem, recv_sem, own_sem
        self.me = lax.axis_index("gx")

    def copy(self, slot, d):
        peer = lax.rem(self.me + d, self.n)
        return pltpu.make_async_remote_copy(
            src_ref=self.source.at[slot, peer],
            dst_ref=self.target.at[slot, self.me],
            send_sem=self.send_sem.at[slot, d],
            recv_sem=self.recv_sem.at[slot, d],
            device_id={"gx": peer},
            device_id_type=MESH,
        )

    def own(self, slot):
        return pltpu.make_async_copy(
            self.source.at[slot, self.me], self.target.at[slot, self.me], self.own_sem.at[slot]
        )

    def start(self, slot):
        def send(d, carry):
            self.copy(slot, d).start()
            return carry

        lax.fori_loop(1, self.n, send, 0, unroll=True)
        self.own(slot).start()

    def wait(self, slot):
        def one(d, carry):
            self.copy(slot, d).wait()
            return carry

        lax.fori_loop(1, self.n, one, 0, unroll=True)
        self.own(slot).wait()


CHUNK = 16
TABLES = 8


def main_kernel(n, tx, txc, *refs):
    refs = list(refs)
    f_hbm, w_hbm, wm_hbm, lift_ref, middle_ref, project_ref = refs[:6]
    table_hbm = refs[6 : 6 + TABLES]
    slab_ref, lifted_ref, base_ref, final_wide = refs[6 + TABLES : 10 + TABLES]
    rest = refs[10 + TABLES :]
    tables = rest[:TABLES]
    (
        f_ref, w_ref, wm_ref, lev_ref, grown_ref, wire_one, got_one, wire_two, got_two,
        modal, mixed, flat_ref, modes_ref, pooled_ref, coarse_ref, stage, got_three, back_c, got_four,
        lift_wide, middle_wide, proj_wide,
        send_one, recv_one, own_one, send_two, recv_two, own_two,
        send_three, recv_three, own_three, send_four, recv_four, own_four,
        f_sem, w_sem, wm_sem, table_sem,
    ) = rest[TABLES:]
    ty_ref, tz_ref, tyi_ref, tzi_ref, yc_ref, zc_ref, zp_ref, perm_ref = tables
    channels, local_x, cells_y, cells_z = f_ref.shape
    modes_x, _, _, owned = w_ref.shape
    modes_y = ty_ref.shape[0] // 2
    per = modes_y // n
    chunks = channels // CHUNK
    rows = local_x * CHUNK
    half = CHUNK // 2
    quad = 4

    me = lax.axis_index("gx")
    barrier = pltpu.get_barrier_semaphore()
    for d in range(1, n):
        pl.semaphore_signal(barrier, 1, device_id={"gx": lax.rem(me + d, n)}, device_id_type=MESH)

    loads = [
        pltpu.make_async_copy(
            f_hbm.at[pl.ds(q * CHUNK, CHUNK)], f_ref.at[pl.ds(q * CHUNK, CHUNK)], f_sem.at[q]
        )
        for q in range(chunks)
    ]
    fills = [
        pltpu.make_async_copy(source, target, table_sem.at[i])
        for i, (source, target) in enumerate(zip(table_hbm, tables))
    ]
    loads[0].start()
    fills[0].start()
    fills[1].start()
    for load in loads[1:]:
        load.start()
    for fill in fills[2:]:
        fill.start()
    fetch = pltpu.make_async_copy(w_hbm, w_ref, w_sem)
    fetch.start()
    fetch_c = pltpu.make_async_copy(wm_hbm, wm_ref, wm_sem)
    fetch_c.start()

    one = Exchange(n, wire_one, got_one, send_one, recv_one, own_one)
    two = Exchange(n, wire_two, got_two, send_two, recv_two, own_two)
    three = Exchange(n, stage, got_three, send_three, recv_three, own_three)
    four = Exchange(n, back_c, got_four, send_four, recv_four, own_four)

    fills[0].wait()
    fills[1].wait()
    tail_lane = lax.broadcasted_iota(jnp.int32, (3 * half, 128), 1) // 32

    def forward(q, carry):
        pltpu.make_async_copy(
            f_hbm.at[pl.ds(q * CHUNK, CHUNK)], f_ref.at[pl.ds(q * CHUNK, CHUNK)], f_sem.at[q]
        ).wait()

        def channel(c, inner):
            wide = jnp.concatenate([f_ref[q * CHUNK + c, x] for x in range(local_x)], 1)
            high, low = split(wide)
            both = dot(ty_ref[...], jnp.concatenate([high, low], 0))
            both = both[:modes_y] + both[modes_y:]
            for x in range(local_x):
                grown_ref[pl.ds(x * CHUNK + c, modes_y, stride=rows), :] = both[
                    :, x * cells_z : (x + 1) * cells_z
                ]
            return inner

        lax.fori_loop(0, CHUNK, channel, 0, unroll=8)

        def owners(b, inner):
            size = quad * per * rows
            done = dot_right3(grown_ref[pl.ds(pl.multiple_of(b * size, 8), size), :], tz_ref[...])
            for k in range(quad):
                part = done[k * per * rows : (k + 1) * per * rows]
                total = jnp.concatenate(
                    [part[g * rows + 3 * half : (g + 1) * rows] for g in range(per)], 0
                )
                for g in range(per):
                    total = jnp.where(tail_lane == g, part[g * rows : g * rows + 3 * half], total)
                wire_one[q, b * quad + k] = total
            return inner

        lax.fori_loop(0, n // quad, owners, 0, unroll=2)

        @pl.when(q == 0)
        def _():
            pl.semaphore_wait(barrier, n - 1)

        one.start(q)
        return carry

    lax.fori_loop(0, chunks, forward, 0)

    widen(lift_ref, ((lift_wide, 0, same),))

    def lift(b, carry):
        at = pl.ds(pl.multiple_of(b * 8, 8), 8)
        store_block(lev_ref, at, dot_left3(lift_wide[...], load_block(f_ref, at)))
        return carry

    lax.fori_loop(0, cells_y // 8, lift, 0)
    mixed[...] = jnp.zeros_like(mixed)
    for fill in fills[2:]:
        fill.wait()
    fetch.wait()
    fetch_c.wait()

    small_lane = lax.broadcasted_iota(jnp.int32, (half, 128), 1) // 32

    def absorb(q, carry):
        one.wait(q)
        for k in range(modes_x):
            first = sum(got_one[q, a, :CHUNK] * np.float32(tx[k, a, 0]) for a in range(n))
            second = sum(got_one[q, a] * np.float32(tx[k, a, 1]) for a in range(n))
            extra = jnp.zeros((half, 128), F32)
            for g in range(3):
                piece = pltpu.roll(second[g * half : (g + 1) * half], 32 * (g + 1), 1)
                extra = jnp.where(small_lane == g, piece, extra)
            total = first + jnp.concatenate([second[CHUNK:], extra], 0)
            modal[k, pl.ds(pl.multiple_of(q * CHUNK, 8), CHUNK)] = total.astype(BF16).astype(F32)

        @pl.when(q < chunks - 1)
        def _():
            def mode(k, inner):
                total = mixed[k, :, :owned]
                for c in range(CHUNK):
                    at = q * CHUNK + c
                    total += modal[k, pl.ds(at, 1), :owned] * w_ref[k, at].astype(F32)
                mixed[k, :, :owned] = total
                return inner

            lax.fori_loop(0, modes_x, mode, 0, unroll=2)

        return carry

    lax.fori_loop(0, chunks, absorb, 0)

    wide_lane = lax.broadcasted_iota(jnp.int32, (3 * half, 128), 1)

    def back(h, carry):
        at = pl.ds(pl.multiple_of(h * CHUNK, CHUNK), CHUNK)

        def mode(k, inner):
            total = mixed[k, at, :owned]
            for c in range(channels - CHUNK, channels):
                total += modal[k, c : c + 1, :owned] * w_ref[k, c, at].astype(F32)
            mixed[k, at, :owned] = total
            return inner

        lax.fori_loop(0, modes_x, mode, 0, unroll=2)
        value = [mixed[k, at] for k in range(modes_x)]
        for a in range(n):
            first = sum(value[k] * np.float32(tx[k, a, 0]) for k in range(modes_x))
            second = sum(value[k] * np.float32(tx[k, a, 1]) for k in range(modes_x))
            rolled = jnp.concatenate(
                [pltpu.roll(second[half:], 96 - 32 * g, 1) for g in range(3)], 0
            )
            wire_two[h, a] = jnp.where(
                wide_lane < 96, jnp.concatenate([first, second[:half]], 0), rolled
            )
        two.start(h)
        return carry

    lax.fori_loop(0, chunks, back, 0)

    size = channels * 8
    widen(middle_ref, ((middle_wide, 0, same),))
    widen(
        project_ref,
        (
            (proj_wide, 0, same),
            (final_wide, 0, lambda left, right: left // 2 == right),
            (final_wide, size, lambda left, right: left // 2 + 4 == right),
        ),
    )

    lane = lax.broadcasted_iota(jnp.int32, (rows, 128), 1) // 32
    tail = lax.broadcasted_iota(jnp.int32, (rows, 128), 0) >= 3 * half
    half_y = cells_y // 2
    modes_c = yc_ref.shape[0] // 2 - half_y
    parts = zc_ref.shape[1] // 128
    narrow = 128 // CHUNK
    coarse_lane = (
        lax.broadcasted_iota(jnp.int32, (modes_c, parts * 128), 1) // narrow % CHUNK
    )
    c_rows = modes_c + half_y

    def middle(h, carry):
        two.wait(h)

        def inverse(b, inner):
            lefts = []
            for k in range(quad):
                a = b * quad + k
                for g in range(per):
                    value = jnp.concatenate(
                        [got_two[h, a], got_two[h, a, g * half : (g + 1) * half]], 0
                    )
                    lefts.append(jnp.where(lane == jnp.where(tail, 3, g), value, 0.0))
            done = dot_right3(jnp.concatenate(lefts, 0), tzi_ref[...])
            size = quad * per * rows
            grown_ref[pl.ds(pl.multiple_of(b * size, 8), size), :] = done
            return inner

        lax.fori_loop(0, n // quad, inverse, 0, unroll=2)

        def level(pair, inner):
            sums = []
            for o in range(2):
                o = 2 * pair + o
                wide = jnp.concatenate(
                    [grown_ref[pl.ds(x * CHUNK + o, modes_y, stride=rows), :] for x in range(local_x)],
                    1,
                )
                done = dot_left3(tyi_ref[...], wide)
                at = h * CHUNK + o
                values = []
                for x in range(local_x):
                    value = gelu(lev_ref[at, x] + done[:, x * cells_z : (x + 1) * cells_z])
                    lev_ref[at, x] = value
                    values.append(value)
                sums.append(values[0] + values[1])
            high, low = split(jnp.concatenate(sums, 1))
            both = dot(yc_ref[...], jnp.concatenate([high, low], 0))
            both = both[:c_rows] + both[c_rows:]
            for o in range(2):
                part = both[:, o * 128 : (o + 1) * 128]
                o = 2 * pair + o
                flat_ref[pl.ds(pl.multiple_of(o * half_y, 8), half_y), :] = part[:half_y]
                modes_ref[pl.ds(pl.multiple_of(o * modes_c, 8), modes_c), :] = part[half_y:]
            return inner

        lax.fori_loop(0, CHUNK // 2, level, 0, unroll=4)

        done = dot_right3(modes_ref[...], zc_ref[...])
        total = jnp.zeros((modes_c, parts * 128), F32)
        for o in range(CHUNK):
            total = jnp.where(coarse_lane == o, done[o * modes_c : (o + 1) * modes_c], total)
        high, low = split(flat_ref[...])
        mean = dot(jnp.concatenate([high, low], 1), zp_ref[...])
        at = pl.ds(h * CHUNK, CHUNK)
        pooled_ref[at] = mean.reshape(CHUNK, half_y, 128)
        for p in range(parts):
            coarse_ref[pl.ds(h * modes_c * parts + p, modes_c, stride=parts), :] = total[
                :, p * 128 : (p + 1) * 128
            ]
        return carry

    lax.fori_loop(0, chunks, middle, 0)

    count = stage.shape[2]
    c_size = modes_c * parts
    for a in range(n):
        for h in range(chunks):
            stage[0, a, :, h * 128 : (h + 1) * 128] = coarse_ref[
                h * c_size + a * count : h * c_size + (a + 1) * count
            ]
    three.start(0)

    def project(b, carry):
        at = pl.ds(pl.multiple_of(b * 8, 8), 8)
        done = dot_left3(proj_wide[...], load_block(lev_ref, at))
        store_block(base_ref, at, load_block(f_ref, at) + done)
        return carry

    blocks = cells_y // 8
    lax.fori_loop(0, blocks // 2, project, 0, unroll=3)
    three.wait(0)
    modes_k = wm_ref.shape[1]
    wave = [
        sum(got_three[0, a] * np.float32(txc[k, a]) for a in range(n)) for k in range(modes_k)
    ]
    wave = jnp.concatenate(wave, 0).astype(BF16)
    turned = dot(wave, perm_ref[:, : wave.shape[1]])
    width = wave.shape[1]
    keep = (
        lax.broadcasted_iota(jnp.int32, (narrow, width), 1) // channels
        == lax.broadcasted_iota(jnp.int32, (narrow, width), 0)
    )
    outs = []
    for k in range(modes_k):
        for t in range(count):
            row = turned[k * count + t : k * count + t + 1]
            left = jnp.where(keep, jnp.broadcast_to(row, (narrow, width)), 0.0).astype(BF16)
            right = wm_ref[t * narrow : (t + 1) * narrow, k].reshape(narrow * channels, channels)
            outs.append(dot(left, right))
    high, low = split(jnp.concatenate(outs, 0))
    spread = perm_ref[: 2 * channels, width:]
    grown = dot(jnp.concatenate([high, low], 1), spread)
    ours = (
        lax.broadcasted_iota(jnp.int32, grown.shape, 1) % narrow
        == lax.broadcasted_iota(jnp.int32, grown.shape, 0) % narrow
    )
    grown = jnp.where(ours, grown, 0.0).reshape(modes_k * count, narrow, width).sum(1)
    for a in range(n):
        back_c[0, a] = sum(
            grown[k * count : (k + 1) * count] * np.float32(txc[k, a]) for k in range(modes_k)
        )
    four.start(0)

    def lift_coarse(g, carry):
        at = [pl.ds(pl.multiple_of(g * 16 + 8 * k, 8), 8) for k in range(2)]
        pooled = jnp.concatenate([pooled_ref[:, a, :].reshape(channels * 8, 128) for a in at], 1)
        done = dot_left3(middle_wide[...], pooled)
        for k in range(2):
            lifted_ref[:, at[k], :] = done[:, k * 128 : (k + 1) * 128].reshape(channels, 8, 128)
        return carry

    lax.fori_loop(0, half_y // 16, lift_coarse, 0)
    lax.fori_loop(blocks // 2, blocks, project, 0, unroll=3)
    four.wait(0)
    for a in range(n):
        for h in range(chunks):
            slab_ref[h * c_size + a * count : h * c_size + (a + 1) * count, :] = got_four[
                0, a, :, h * 128 : (h + 1) * 128
            ]


def main_call(n, tx, txc, features, weights, middle_weights, matrices, tables):
    channels, local_x, cells_y, cells_z = features.shape
    turned = jnp.transpose(weights, (1, 2, 3, 0))
    modes_x = turned.shape[0]
    size = channels * 8
    chunks = channels // CHUNK
    wire = (chunks, n, 3 * CHUNK // 2, 128)
    c_rows = (KY // 2) * (KZ // 2) // (128 // CHUNK)
    coarse = (1, n, c_rows // n, channels * 128 // CHUNK)
    wide = (size, 3 * size)

    def sems(slots):
        return [
            pltpu.SemaphoreType.DMA((slots, n)),
            pltpu.SemaphoreType.DMA((slots, n)),
            pltpu.SemaphoreType.DMA((slots,)),
        ]

    return pl.pallas_call(
        functools.partial(main_kernel, n, tx, txc),
        out_shape=(
            pltpu.VMEM((c_rows * chunks, 128), F32),
            pltpu.VMEM((channels, cells_y // 2, 128), F32),
            pltpu.VMEM(features.shape, F32),
            pltpu.VMEM((2 * size, 3 * size), BF16),
        ),
        in_specs=[far()] * 3 + [whole()] * 3 + [far()] * TABLES,
        out_specs=(whole(),) * 4,
        scratch_shapes=[pltpu.VMEM(table.shape, table.dtype) for table in tables]
        + [
            pltpu.VMEM(features.shape, F32),
            pltpu.VMEM(turned.shape, BF16),
            pltpu.VMEM(middle_weights.shape, BF16),
            pltpu.VMEM(features.shape, F32),
            pltpu.VMEM((KY * local_x * CHUNK, cells_z), F32),
            pltpu.VMEM(wire, F32),
            pltpu.VMEM(wire, F32),
            pltpu.VMEM(wire, F32),
            pltpu.VMEM(wire, F32),
            pltpu.VMEM((modes_x, channels, 128), F32),
            pltpu.VMEM((modes_x, channels, 128), F32),
            pltpu.VMEM((CHUNK * cells_y // 2, 128), F32),
            pltpu.VMEM((CHUNK * KY // 2, 128), F32),
            pltpu.VMEM((channels, cells_y // 2, 128), F32),
            pltpu.VMEM((c_rows * chunks, 128), F32),
            pltpu.VMEM(coarse, F32),
            pltpu.VMEM(coarse, F32),
            pltpu.VMEM(coarse, F32),
            pltpu.VMEM(coarse, F32),
            pltpu.VMEM(wide, BF16),
            pltpu.VMEM(wide, BF16),
            pltpu.VMEM(wide, BF16),
        ]
        + sems(chunks)
        + sems(chunks)
        + sems(1)
        + sems(1)
        + [
            pltpu.SemaphoreType.DMA((chunks,)),
            pltpu.SemaphoreType.DMA,
            pltpu.SemaphoreType.DMA,
            pltpu.SemaphoreType.DMA((TABLES,)),
        ],
        compiler_params=pltpu.CompilerParams(
            collective_id=0, has_side_effects=True, vmem_limit_bytes=48 * 1024 * 1024
        ),
        name="main",
    )(features, turned, middle_weights, *matrices, *tables)


def final_kernel(
    slab_ref, ty_hbm, tz_hbm, lifted_ref, proj_ref, base_ref, out_hbm,
    ty_ref, tz_ref, sum_ref, spec_ref, load_sem, save_sem,
):
    loads = [
        pltpu.make_async_copy(source, target, load_sem.at[i])
        for i, (source, target) in enumerate(
            ((ty_hbm, ty_ref), (tz_hbm, tz_ref))
        )
    ]
    for load in loads:
        load.start()
    for load in loads:
        load.wait()
    channels, half_y, _ = lifted_ref.shape
    local_x = base_ref.shape[1]
    modes = ty_ref.shape[1] // 3
    parts = tz_ref.shape[0] // (3 * 128)
    chunks = channels // CHUNK
    c_size = modes * parts
    stacked = []
    for h in range(chunks):
        wide = jnp.concatenate(
            [slab_ref[pl.ds(h * c_size + p, modes, stride=parts), :] for p in range(parts)], 1
        )
        stacked.append(dot_left3(ty_ref[...], wide))
    grown = jnp.concatenate(stacked, 0)
    high, low = split(grown)
    left = jnp.concatenate([high, low, high], 1)
    lane = lax.broadcasted_iota(jnp.int32, left.shape, 1) // (128 // CHUNK) % CHUNK

    for c in range(CHUNK):
        done = dot(jnp.where(lane == c, left, jnp.zeros_like(left)), tz_ref[...])
        for h in range(chunks):
            spec_ref[h * CHUNK + c] = done[h * half_y : (h + 1) * half_y]

    saves = []
    for g in range(half_y // 16):
        at = [pl.ds(g * 16 + 8 * k, 8) for k in range(2)]
        pooled = jnp.concatenate([lifted_ref[:, a, :].reshape(channels * 8, 128) for a in at], 1)
        spectral = jnp.concatenate([spec_ref[:, a, :].reshape(channels * 8, 128) for a in at], 1)
        added = dot_left3(proj_ref[...], gelu(pooled + spectral))
        for k in range(2):
            for b in range(2):
                piece = added[b * channels * 8 : (b + 1) * channels * 8, k * 128 : (k + 1) * 128]
                piece = piece.reshape(channels, 8, 128)
                rows = pl.ds(g * 32 + 16 * k + 8 * b, 8)
                for x in range(local_x):
                    sum_ref[:, x, rows, :] = base_ref[:, x, rows, :] + piece
        rows = pl.ds(g * 32, 32)
        save = pltpu.make_async_copy(
            sum_ref.at[:, :, rows, :], out_hbm.at[:, :, rows, :], save_sem.at[g]
        )
        save.start()
        saves.append(save)
    for save in saves:
        save.wait()


def on_device(features, fine_weights, middle_weights, lift_fine, lift_middle, project_out):
    channels, local_x, cells_y, cells_z = features.shape
    n = lax.axis_size("gx")
    owned = fine_weights.shape[0]
    owned_c = middle_weights.shape[0]
    half_ky, half_kz = KY // 2, KZ // 2
    narrow = 128 // CHUNK
    fits = (
        owned == 3 * KZ
        and KZ == 32
        and KY == 3 * n
        and n % 4 == 0
        and owned_c % narrow == 0
        and local_x == 2
        and cells_z == 128
        and cells_y % 32 == 0
        and channels == 3 * CHUNK
    )
    if not fits:
        return general_device(
            features, fine_weights, middle_weights, lift_fine, lift_middle, project_out
        )
    modes_x = fine_weights.shape[1]
    modes_c = middle_weights.shape[1]
    tx = np.asarray(host_table(modes_x, local_x * n), np.float32).reshape(modes_x, n, local_x)
    txc = np.asarray(host_table(modes_c, n), np.float32)

    half_y, half_z = cells_y // 2, cells_z // 2
    pool_y = np.repeat(np.eye(half_y), 2, axis=1) * 0.5
    pool_z = np.repeat(np.eye(half_z), 2, axis=1) * 0.25
    ty_c = host_table(half_ky, half_y)
    tz_c = host_table(half_kz, half_z)
    parts = half_kz // narrow
    chunks = channels // CHUNK
    ty = left_rows(host_table(KY, cells_y))
    tz = right_three(np.tile(host_table(KZ, cells_z).T, (1, 4)))
    yc = left_rows(np.concatenate([pool_y, ty_c @ pool_y], 0))
    zc_full = (tz_c @ pool_z).T.reshape(cells_z, parts, 1, narrow)
    zc = right_three(np.broadcast_to(zc_full, (cells_z, parts, CHUNK, narrow)).reshape(cells_z, -1))
    zp = np.repeat(pool_z, 2, axis=0).T
    zp = np.asarray(zp, jnp.bfloat16)
    zp = jnp.asarray(np.concatenate([zp, zp], 0))
    ty_i = left_three(host_table(KY, cells_y).T)
    tz_i = right_three(np.tile(host_table(KZ, cells_z), (4, 1)))
    width = channels * narrow
    turn = np.zeros((width, 2 * width), np.float32)
    for c in range(channels):
        for j in range(narrow):
            turn[c * narrow + j, j * channels + c] = 1.0
            turn[c, width + c * narrow + j] = 1.0
            turn[channels + c, width + c * narrow + j] = 1.0
    turn = jnp.asarray(turn.astype(jnp.bfloat16))
    slab, lifted, base, projm = main_call(
        n, tx, txc, features, fine_weights, middle_weights,
        (lift_fine, lift_middle, project_out), (ty, tz, ty_i, tz_i, yc, zc, zp, turn),
    )

    tyc_i = left_three(ty_c.T)
    grown = np.repeat(tz_c, 2, axis=1).reshape(parts, 1, narrow, cells_z)
    tzc_i = right_three(np.broadcast_to(grown, (parts, CHUNK, narrow, cells_z)).reshape(-1, cells_z))
    return pl.pallas_call(
        final_kernel,
        out_shape=jax.ShapeDtypeStruct(features.shape, F32),
        in_specs=[whole(), far(), far(), whole(), whole(), whole()],
        out_specs=far(),
        scratch_shapes=[
            pltpu.VMEM(tyc_i.shape, tyc_i.dtype),
            pltpu.VMEM(tzc_i.shape, tzc_i.dtype),
            pltpu.VMEM(features.shape, F32),
            pltpu.VMEM((channels, half_y, 128), F32),
            pltpu.SemaphoreType.DMA((2,)),
            pltpu.SemaphoreType.DMA((half_y // 16,)),
        ],
        compiler_params=pltpu.CompilerParams(vmem_limit_bytes=24 * 1024 * 1024),
        name="final",
    )(slab, tyc_i, tzc_i, lifted, projm, base)


def solution(mesh):
    in_specs = (
        P(None, ("groups", "gx"), None, None),
        P("gx", None, None, None),
        P("gx", None, None, None),
        P(),
        P(),
        P(),
    )
    out_specs = P(None, ("groups", "gx"), None, None)
    return jax.shard_map(
        on_device, mesh=mesh, in_specs=in_specs, out_specs=out_specs, check_vma=False
    )
```

```python
import functools

import jax
import jax.numpy as jnp
import numpy as np
from jax import lax
from jax.experimental import pallas as pl
from jax.experimental.pallas import tpu as pltpu
from jax.sharding import PartitionSpec as P

KY = 48
KZ = 32


HIGHEST = lax.Precision.HIGHEST


def cosine_table(modes_kept, length, columns):
    orders = jnp.arange(modes_kept, dtype=jnp.int32)[:, None]
    points = jnp.arange(columns, dtype=jnp.int32)[None, :]
    phase = orders * (2 * points + 1) % (4 * length)
    angle = jnp.pi / (2 * length) * phase.astype(jnp.float32)
    scales = jnp.where(
        orders == 0, jnp.sqrt(jnp.float32(1.0 / length)), jnp.sqrt(jnp.float32(2.0 / length))
    )
    return scales * jnp.cos(angle)


def forward_yz(values, modes_y, modes_z):
    channels, local_x, cells_y, cells_z = values.shape
    table_z = cosine_table(modes_z, cells_z, cells_z)
    table_y = cosine_table(modes_y, cells_y, cells_y)
    along_z = jnp.einsum("cxyz,jz->cxyj", values, table_z, precision=HIGHEST)
    both = jnp.einsum("cxyj,iy->ijxc", along_z, table_y, precision=HIGHEST)
    return both.reshape(modes_y * modes_z, local_x, channels)


def inverse_yz(coeffs, modes_y, modes_z, cells_y, cells_z):
    total, local_x, channels = coeffs.shape
    shaped = coeffs.reshape(modes_y, modes_z, local_x, channels)
    table_z = cosine_table(modes_z, cells_z, cells_z)
    table_y = cosine_table(modes_y, cells_y, cells_y)
    along_y = jnp.einsum("ijxc,iy->jxcy", shaped, table_y, precision=HIGHEST)
    return jnp.einsum("jxcy,jz->cxyz", along_y, table_z, precision=HIGHEST)


def mix_modes(modal, weights):
    return jnp.einsum(
        "mkc,mkco->mko", modal.astype(jnp.bfloat16), weights, preferred_element_type=jnp.float32
    )


def pointwise(values, matrix):
    return jnp.einsum("cxyz,co->oxyz", values, matrix, precision=HIGHEST)


def coarsen(values):
    channels, cells_x, cells_y, cells_z = values.shape
    shaped = values.reshape(channels, cells_x // 2, 2, cells_y // 2, 2, cells_z // 2, 2)
    return jnp.mean(shaped, axis=(2, 4, 6))


def refine(values):
    return jnp.repeat(jnp.repeat(jnp.repeat(values, 2, axis=1), 2, axis=2), 2, axis=3)


def general_device(features, fine_weights, middle_weights, lift_fine, lift_middle, project_out):
    channels, local_x, cells_y, cells_z = features.shape
    group_size = lax.axis_size("gx")
    cells_x = local_x * group_size
    modes_x = fine_weights.shape[1]
    coeffs = forward_yz(features, KY, KZ)
    table_x = cosine_table(modes_x, cells_x, cells_x)
    owned_pairs = coeffs.shape[0] // group_size
    grouped = coeffs.reshape(group_size, owned_pairs, local_x, channels)
    modal = jnp.einsum(
        "amxc,kx->mkc",
        lax.all_to_all(grouped, "gx", split_axis=0, concat_axis=2, tiled=True),
        table_x,
        precision=HIGHEST,
    )
    mixed = mix_modes(modal, fine_weights)
    back = jnp.einsum("mkc,kx->mxc", mixed, table_x, precision=HIGHEST)
    slabs = lax.all_to_all(back, "gx", split_axis=1, concat_axis=0, tiled=True)
    level_one = jax.nn.gelu(
        inverse_yz(slabs, KY, KZ, cells_y, cells_z) + pointwise(features, lift_fine),
        approximate=False,
    )
    pooled = coarsen(level_one)
    half_x = local_x // 2
    half_ky = KY // 2
    half_kz = KZ // 2
    half_modes = middle_weights.shape[1]
    coarse_x = half_x * group_size
    coarse_coeffs = forward_yz(pooled, half_ky, half_kz)
    coarse_pencils = lax.all_to_all(coarse_coeffs, "gx", split_axis=0, concat_axis=1, tiled=True)
    coarse_table = cosine_table(half_modes, coarse_x, coarse_x)
    coarse_modal = jnp.einsum("mxc,kx->mkc", coarse_pencils, coarse_table, precision=HIGHEST)
    coarse_mixed = mix_modes(coarse_modal, middle_weights)
    coarse_back = jnp.einsum("mkc,kx->mxc", coarse_mixed, coarse_table, precision=HIGHEST)
    coarse_slabs = lax.all_to_all(coarse_back, "gx", split_axis=1, concat_axis=0, tiled=True)
    level_two = jax.nn.gelu(
        inverse_yz(coarse_slabs, half_ky, half_kz, cells_y // 2, cells_z // 2)
        + pointwise(pooled, lift_middle),
        approximate=False,
    )
    return features + pointwise(level_one + refine(level_two), project_out)


BF16 = jnp.bfloat16
MESH = pl.DeviceIdType.MESH
F32 = jnp.float32


def host_table(modes_kept, length):
    orders = np.arange(modes_kept)[:, None]
    points = np.arange(length)[None, :]
    scales = np.where(orders == 0, np.sqrt(1.0 / length), np.sqrt(2.0 / length))
    return scales * np.cos(np.pi * orders * (2 * points + 1) / (2 * length))


def host_split(table):
    table = np.asarray(table, np.float32)
    high = table.astype(jnp.bfloat16)
    low = (table - high.astype(np.float32)).astype(jnp.bfloat16)
    return high, low


def left_rows(table):
    high, low = host_split(table)
    return jnp.asarray(
        np.concatenate([np.concatenate([high, high], 1), np.concatenate([low, low], 1)], 0)
    )


def left_three(table):
    high, low = host_split(table)
    return jnp.asarray(np.concatenate([high, high, low], 1))


def right_three(table):
    high, low = host_split(table)
    return jnp.asarray(np.concatenate([high, high, low], 0))


def split(values):
    high = values.astype(BF16)
    low = (values - high.astype(F32)).astype(BF16)
    return high, low


def dot(left, right):
    return jnp.dot(left, right, preferred_element_type=F32)


def dot_left3(left3, values):
    high, low = split(values)
    return dot(left3, jnp.concatenate([high, low, high], 0))


def dot_right3(values, right3):
    high, low = split(values)
    return dot(jnp.concatenate([high, low, high], 1), right3)


def gelu(t):
    return 0.5 * t * (1.0 + lax.erf(t * np.float32(np.sqrt(0.5))))


def far():
    return pl.BlockSpec(memory_space=pl.ANY)


def whole():
    return pl.BlockSpec(memory_space=pltpu.VMEM)


def widen(matrix_ref, targets):
    channels = matrix_ref.shape[0]
    size = channels * 8
    row = lax.broadcasted_iota(jnp.int32, (size, channels), 0) // 8
    pick = (row == lax.broadcasted_iota(jnp.int32, (size, channels), 1)).astype(F32).astype(BF16)
    col = lax.broadcasted_iota(jnp.int32, (channels, size), 1) // 8
    place = (col == lax.broadcasted_iota(jnp.int32, (channels, size), 0)).astype(F32).astype(BF16)
    left = lax.broadcasted_iota(jnp.int32, (size, size), 0) % 8
    right = lax.broadcasted_iota(jnp.int32, (size, size), 1) % 8
    for part, spots in zip(split(matrix_ref[...]), ((0, 1), (2,))):
        grown = lax.dot_general(pick, part, (((1,), (1,)), ((), ())), preferred_element_type=F32)
        grown = dot(grown.astype(BF16), place)
        for ref, at, rule in targets:
            value = jnp.where(rule(left, right), grown, 0.0).astype(BF16)
            for spot in spots:
                ref[at : at + size, spot * size : (spot + 1) * size] = value


def same(left, right):
    return left == right


def load_block(ref, at):
    channels, local_x, _, cells_z = ref.shape
    return jnp.concatenate([ref[:, x, at, :].reshape(channels * 8, cells_z) for x in range(local_x)], 1)


def store_block(ref, at, value):
    channels, local_x, _, cells_z = ref.shape
    for x in range(local_x):
        ref[:, x, at, :] = value[:, x * cells_z : (x + 1) * cells_z].reshape(channels, 8, cells_z)


def greet(n):
    me = lax.axis_index("gx")
    barrier = pltpu.get_barrier_semaphore()
    for d in range(1, n):
        pl.semaphore_signal(barrier, 1, device_id={"gx": lax.rem(me + d, n)}, device_id_type=MESH)
    pl.semaphore_wait(barrier, n - 1)


class Exchange:
    def __init__(self, n, parts, source, target, send_sem, recv_sem, own_sem):
        self.n, self.parts, self.source, self.target = n, parts, source, target
        self.send_sem, self.recv_sem, self.own_sem = send_sem, recv_sem, own_sem
        self.me = lax.axis_index("gx")

    def copy(self, part, d):
        peer = jnp.bitwise_xor(self.me, d)
        rows = pl.ds(*self.parts[part])
        return pltpu.make_async_remote_copy(
            src_ref=self.source.at[peer, rows],
            dst_ref=self.target.at[self.me, rows],
            send_sem=self.send_sem.at[part, d],
            recv_sem=self.recv_sem.at[part, d],
            device_id={"gx": peer},
            device_id_type=MESH,
        )

    def own(self, part):
        rows = pl.ds(*self.parts[part])
        return pltpu.make_async_copy(
            self.source.at[self.me, rows], self.target.at[self.me, rows], self.own_sem.at[part]
        )

    def start(self, part):
        for d in range(self.n - 1, 0, -1):
            self.copy(part, d).start()
        self.own(part).start()

    def wait(self, part):
        for d in range(1, self.n):
            self.copy(part, d).wait()
        self.own(part).wait()

    def after(self, q, action):
        for part, chunks in enumerate(self.chunks):
            last = chunks[-1] if action == self.start else chunks[0]
            pl.when(q == last)(functools.partial(action, part))


OUT = ((0,), (1, 2))
BACK = ((0,), (1,), (2,))


def chunk_exchange(n, plan, *refs):
    rows = 3 * CHUNK // 2
    parts = [(chunks[0] * rows, len(chunks) * rows) for chunks in plan]
    exchange = Exchange(n, parts, *refs)
    exchange.chunks = plan
    return exchange


CHUNK = 16
TABLES = 8


def main_kernel(n, tx, txc, *refs):
    refs = list(refs)
    f_hbm, w_hbm, wm_hbm = refs[:3]
    matrix_hbm = refs[3:6]
    table_hbm = refs[6 : 6 + TABLES]
    slab_ref, lifted_ref, base_ref, final_wide = refs[6 + TABLES : 10 + TABLES]
    rest = refs[10 + TABLES :]
    tables = rest[:TABLES]
    (
        f_ref, w_ref, wm_ref, lev_ref, grown_ref, wire_one, got_one, wire_two, got_two,
        modal, mixed, flat_ref, modes_ref, pooled_ref, coarse_ref, stage, got_three, back_c, got_four,
        lift_wide, middle_wide, proj_wide, lift_ref, middle_ref, project_ref,
        send_one, recv_one, own_one, send_two, recv_two, own_two,
        send_three, recv_three, own_three, send_four, recv_four, own_four,
        f_sem, w_sem, wm_sem, table_sem, matrix_sem,
    ) = rest[TABLES:]
    ty_ref, tz_ref, tyi_ref, tzi_ref, yc_ref, zc_ref, zp_ref, perm_ref = tables
    channels, local_x, cells_y, cells_z = f_ref.shape
    modes_x, _, _, owned = w_ref.shape
    modes_y = ty_ref.shape[0] // 2
    per = modes_y // n
    chunks = channels // CHUNK
    rows = local_x * CHUNK
    half = CHUNK // 2
    quad = 4
    size_q = 3 * half

    def at_chunk(q):
        return pl.ds(pl.multiple_of(q * size_q, 8), size_q)

    me = lax.axis_index("gx")
    barrier = pltpu.get_barrier_semaphore()
    for d in range(1, n):
        pl.semaphore_signal(barrier, 1, device_id={"gx": lax.rem(me + d, n)}, device_id_type=MESH)

    loads = [
        pltpu.make_async_copy(
            f_hbm.at[pl.ds(q * CHUNK, CHUNK)], f_ref.at[pl.ds(q * CHUNK, CHUNK)], f_sem.at[q]
        )
        for q in range(chunks)
    ]
    fills = [
        pltpu.make_async_copy(source, target, table_sem.at[i])
        for i, (source, target) in enumerate(zip(table_hbm, tables))
    ]
    fills += [
        pltpu.make_async_copy(source, target, matrix_sem.at[i])
        for i, (source, target) in enumerate(
            zip(matrix_hbm, (lift_ref, middle_ref, project_ref))
        )
    ]
    loads[0].start()
    fills[0].start()
    fills[1].start()
    for load in loads[1:]:
        load.start()
    for fill in fills[2:]:
        fill.start()
    fetch = pltpu.make_async_copy(w_hbm, w_ref, w_sem)
    fetch_c = pltpu.make_async_copy(wm_hbm, wm_ref, wm_sem)

    one = chunk_exchange(n, OUT, wire_one, got_one, send_one, recv_one, own_one)
    two = chunk_exchange(n, BACK, wire_two, got_two, send_two, recv_two, own_two)
    small = [(0, stage.shape[1])]
    three = Exchange(n, small, stage, got_three, send_three, recv_three, own_three)
    four = Exchange(n, small, back_c, got_four, send_four, recv_four, own_four)

    fills[0].wait()
    fills[1].wait()
    tail_lane = lax.broadcasted_iota(jnp.int32, (3 * half, 128), 1) // 32

    def forward(q, carry):
        pltpu.make_async_copy(
            f_hbm.at[pl.ds(q * CHUNK, CHUNK)], f_ref.at[pl.ds(q * CHUNK, CHUNK)], f_sem.at[q]
        ).wait()

        def channel(c, inner):
            wide = jnp.concatenate([f_ref[q * CHUNK + c, x] for x in range(local_x)], 1)
            high, low = split(wide)
            both = dot(ty_ref[...], jnp.concatenate([high, low], 0))
            both = both[:modes_y] + both[modes_y:]
            for x in range(local_x):
                grown_ref[pl.ds(x * CHUNK + c, modes_y, stride=rows), :] = both[
                    :, x * cells_z : (x + 1) * cells_z
                ]
            return inner

        lax.fori_loop(0, CHUNK, channel, 0, unroll=8)

        def owners(b, inner):
            size = quad * per * rows
            done = dot_right3(grown_ref[pl.ds(pl.multiple_of(b * size, 8), size), :], tz_ref[...])
            for k in range(quad):
                part = done[k * per * rows : (k + 1) * per * rows]
                total = jnp.concatenate(
                    [part[g * rows + 3 * half : (g + 1) * rows] for g in range(per)], 0
                )
                for g in range(per):
                    total = jnp.where(tail_lane == g, part[g * rows : g * rows + 3 * half], total)
                wire_one[b * quad + k, at_chunk(q)] = total
            return inner

        lax.fori_loop(0, n // quad, owners, 0, unroll=2)

        @pl.when(q == 0)
        def _():
            pl.semaphore_wait(barrier, n - 1)

        one.after(q, one.start)
        return carry

    lax.fori_loop(0, chunks, forward, 0)
    fetch.start()
    fetch_c.start()

    for fill in fills[2:]:
        fill.wait()
    widen(lift_ref, ((lift_wide, 0, same),))

    def lift(b, carry):
        at = pl.ds(pl.multiple_of(b * 8, 8), 8)
        store_block(lev_ref, at, dot_left3(lift_wide[...], load_block(f_ref, at)))
        return carry

    lax.fori_loop(0, cells_y // 8, lift, 0)
    mixed[...] = jnp.zeros_like(mixed)
    fetch.wait()
    fetch_c.wait()

    small_lane = lax.broadcasted_iota(jnp.int32, (half, 128), 1) // 32

    def absorb(q, carry):
        one.after(q, one.wait)
        for k in range(modes_x):
            first = sum(got_one[a, pl.ds(pl.multiple_of(q * size_q, 8), CHUNK)] * np.float32(tx[k, a, 0]) for a in range(n))
            second = sum(got_one[a, at_chunk(q)] * np.float32(tx[k, a, 1]) for a in range(n))
            extra = jnp.zeros((half, 128), F32)
            for g in range(3):
                piece = pltpu.roll(second[g * half : (g + 1) * half], 32 * (g + 1), 1)
                extra = jnp.where(small_lane == g, piece, extra)
            total = first + jnp.concatenate([second[CHUNK:], extra], 0)
            modal[k, pl.ds(pl.multiple_of(q * CHUNK, 8), CHUNK)] = total.astype(BF16).astype(F32)

        @pl.when(q < chunks - 1)
        def _():
            def mode(k, inner):
                total = mixed[k, :, :owned]
                for c in range(CHUNK):
                    at = q * CHUNK + c
                    total += modal[k, pl.ds(at, 1), :owned] * w_ref[k, at].astype(F32)
                mixed[k, :, :owned] = total
                return inner

            lax.fori_loop(0, modes_x, mode, 0, unroll=2)

        return carry

    lax.fori_loop(0, chunks, absorb, 0)

    wide_lane = lax.broadcasted_iota(jnp.int32, (3 * half, 128), 1)

    def back(h, carry):
        at = pl.ds(pl.multiple_of(h * CHUNK, CHUNK), CHUNK)

        def mode(k, inner):
            total = mixed[k, at, :owned]
            for c in range(channels - CHUNK, channels):
                total += modal[k, c : c + 1, :owned] * w_ref[k, c, at].astype(F32)
            mixed[k, at, :owned] = total
            return inner

        lax.fori_loop(0, modes_x, mode, 0, unroll=2)
        value = [mixed[k, at] for k in range(modes_x)]
        for a in range(n):
            first = sum(value[k] * np.float32(tx[k, a, 0]) for k in range(modes_x))
            second = sum(value[k] * np.float32(tx[k, a, 1]) for k in range(modes_x))
            rolled = jnp.concatenate(
                [pltpu.roll(second[half:], 96 - 32 * g, 1) for g in range(3)], 0
            )
            wire_two[a, at_chunk(h)] = jnp.where(
                wide_lane < 96, jnp.concatenate([first, second[:half]], 0), rolled
            )
        two.after(h, two.start)
        return carry

    lax.fori_loop(0, chunks, back, 0)

    size = channels * 8
    widen(middle_ref, ((middle_wide, 0, same),))
    widen(
        project_ref,
        (
            (proj_wide, 0, same),
            (final_wide, 0, lambda left, right: left // 2 == right),
            (final_wide, size, lambda left, right: left // 2 + 4 == right),
        ),
    )

    half_y = cells_y // 2
    modes_c = yc_ref.shape[0] // 2 - half_y
    parts = zc_ref.shape[1] // 128
    narrow = 128 // CHUNK
    coarse_lane = (
        lax.broadcasted_iota(jnp.int32, (modes_c, parts * 128), 1) // narrow % CHUNK
    )
    c_rows = modes_c + half_y

    def middle(h, carry):
        two.after(h, two.wait)

        def inverse(b, inner):
            values = [got_two[b * quad + k, at_chunk(h)] for k in range(quad)]
            done = dot_right3(jnp.concatenate(values, 0), tzi_ref[...])
            pieces = []
            for k in range(quad):
                part = done[k * size_q : (k + 1) * size_q]
                for g in range(per):
                    pieces.append(part[:, g * 128 : (g + 1) * 128])
                    pieces.append(part[g * half : (g + 1) * half, per * 128 :])
            size = quad * per * rows
            grown_ref[pl.ds(pl.multiple_of(b * size, 8), size), :] = jnp.concatenate(pieces, 0)
            return inner

        lax.fori_loop(0, n // quad, inverse, 0, unroll=2)

        def level(pair, inner):
            sums = []
            for o in range(2):
                o = 2 * pair + o
                wide = jnp.concatenate(
                    [grown_ref[pl.ds(x * CHUNK + o, modes_y, stride=rows), :] for x in range(local_x)],
                    1,
                )
                done = dot_left3(tyi_ref[...], wide)
                at = h * CHUNK + o
                values = []
                for x in range(local_x):
                    value = gelu(lev_ref[at, x] + done[:, x * cells_z : (x + 1) * cells_z])
                    lev_ref[at, x] = value
                    values.append(value)
                sums.append(values[0] + values[1])
            high, low = split(jnp.concatenate(sums, 1))
            both = dot(yc_ref[...], jnp.concatenate([high, low], 0))
            both = both[:c_rows] + both[c_rows:]
            for o in range(2):
                part = both[:, o * 128 : (o + 1) * 128]
                o = 2 * pair + o
                flat_ref[pl.ds(pl.multiple_of(o * half_y, 8), half_y), :] = part[:half_y]
                modes_ref[pl.ds(pl.multiple_of(o * modes_c, 8), modes_c), :] = part[half_y:]
            return inner

        lax.fori_loop(0, CHUNK // 2, level, 0, unroll=4)

        done = dot_right3(modes_ref[...], zc_ref[...])
        total = jnp.zeros((modes_c, parts * 128), F32)
        for o in range(CHUNK):
            total = jnp.where(coarse_lane == o, done[o * modes_c : (o + 1) * modes_c], total)
        high, low = split(flat_ref[...])
        mean = dot(jnp.concatenate([high, low], 1), zp_ref[...])
        at = pl.ds(h * CHUNK, CHUNK)
        pooled_ref[at] = mean.reshape(CHUNK, half_y, 128)
        for p in range(parts):
            coarse_ref[pl.ds(h * modes_c * parts + p, modes_c, stride=parts), :] = total[
                :, p * 128 : (p + 1) * 128
            ]
        return carry

    lax.fori_loop(0, chunks, middle, 0)

    count = stage.shape[1]
    c_size = modes_c * parts
    for a in range(n):
        for h in range(chunks):
            stage[a, :, h * 128 : (h + 1) * 128] = coarse_ref[
                h * c_size + a * count : h * c_size + (a + 1) * count
            ]
    three.start(0)

    def project(b, carry):
        at = pl.ds(pl.multiple_of(b * 8, 8), 8)
        done = dot_left3(proj_wide[...], load_block(lev_ref, at))
        store_block(base_ref, at, load_block(f_ref, at) + done)
        return carry

    blocks = cells_y // 8
    lax.fori_loop(0, blocks // 2, project, 0, unroll=3)
    three.wait(0)
    modes_k = wm_ref.shape[1]
    wave = [
        sum(got_three[a] * np.float32(txc[k, a]) for a in range(n)) for k in range(modes_k)
    ]
    wave = jnp.concatenate(wave, 0).astype(BF16)
    turned = dot(wave, perm_ref[:, : wave.shape[1]])
    width = wave.shape[1]
    keep = (
        lax.broadcasted_iota(jnp.int32, (narrow, width), 1) // channels
        == lax.broadcasted_iota(jnp.int32, (narrow, width), 0)
    )
    outs = []
    for k in range(modes_k):
        for t in range(count):
            row = turned[k * count + t : k * count + t + 1]
            left = jnp.where(keep, jnp.broadcast_to(row, (narrow, width)), 0.0).astype(BF16)
            right = wm_ref[t * narrow : (t + 1) * narrow, k].reshape(narrow * channels, channels)
            outs.append(dot(left, right))
    high, low = split(jnp.concatenate(outs, 0))
    spread = perm_ref[: 2 * channels, width:]
    grown = dot(jnp.concatenate([high, low], 1), spread)
    ours = (
        lax.broadcasted_iota(jnp.int32, grown.shape, 1) % narrow
        == lax.broadcasted_iota(jnp.int32, grown.shape, 0) % narrow
    )
    grown = jnp.where(ours, grown, 0.0).reshape(modes_k * count, narrow, width).sum(1)
    for a in range(n):
        back_c[a] = sum(
            grown[k * count : (k + 1) * count] * np.float32(txc[k, a]) for k in range(modes_k)
        )
    four.start(0)

    def lift_coarse(g, carry):
        at = [pl.ds(pl.multiple_of(g * 16 + 8 * k, 8), 8) for k in range(2)]
        pooled = jnp.concatenate([pooled_ref[:, a, :].reshape(channels * 8, 128) for a in at], 1)
        done = dot_left3(middle_wide[...], pooled)
        for k in range(2):
            lifted_ref[:, at[k], :] = done[:, k * 128 : (k + 1) * 128].reshape(channels, 8, 128)
        return carry

    lax.fori_loop(0, half_y // 16, lift_coarse, 0)
    lax.fori_loop(blocks // 2, blocks, project, 0, unroll=3)
    four.wait(0)
    for a in range(n):
        for h in range(chunks):
            slab_ref[h * c_size + a * count : h * c_size + (a + 1) * count, :] = got_four[
                a, :, h * 128 : (h + 1) * 128
            ]


def main_call(n, tx, txc, features, weights, middle_weights, matrices, tables):
    channels, local_x, cells_y, cells_z = features.shape
    turned = jnp.transpose(weights, (1, 2, 3, 0))
    modes_x = turned.shape[0]
    size = channels * 8
    chunks = channels // CHUNK
    wire = (n, chunks * 3 * CHUNK // 2, 128)
    c_rows = (KY // 2) * (KZ // 2) // (128 // CHUNK)
    coarse = (n, c_rows // n, channels * 128 // CHUNK)
    wide = (size, 3 * size)

    def sems(slots):
        return [
            pltpu.SemaphoreType.DMA((slots, n)),
            pltpu.SemaphoreType.DMA((slots, n)),
            pltpu.SemaphoreType.DMA((slots,)),
        ]

    return pl.pallas_call(
        functools.partial(main_kernel, n, tx, txc),
        out_shape=(
            pltpu.VMEM((c_rows * chunks, 128), F32),
            pltpu.VMEM((channels, cells_y // 2, 128), F32),
            pltpu.VMEM(features.shape, F32),
            pltpu.VMEM((2 * size, 3 * size), BF16),
        ),
        in_specs=[far()] * (6 + TABLES),
        out_specs=(whole(),) * 4,
        scratch_shapes=[pltpu.VMEM(table.shape, table.dtype) for table in tables]
        + [
            pltpu.VMEM(features.shape, F32),
            pltpu.VMEM(turned.shape, BF16),
            pltpu.VMEM(middle_weights.shape, BF16),
            pltpu.VMEM(features.shape, F32),
            pltpu.VMEM((KY * local_x * CHUNK, cells_z), F32),
            pltpu.VMEM(wire, F32),
            pltpu.VMEM(wire, F32),
            pltpu.VMEM(wire, F32),
            pltpu.VMEM(wire, F32),
            pltpu.VMEM((modes_x, channels, 128), F32),
            pltpu.VMEM((modes_x, channels, 128), F32),
            pltpu.VMEM((CHUNK * cells_y // 2, 128), F32),
            pltpu.VMEM((CHUNK * KY // 2, 128), F32),
            pltpu.VMEM((channels, cells_y // 2, 128), F32),
            pltpu.VMEM((c_rows * chunks, 128), F32),
            pltpu.VMEM(coarse, F32),
            pltpu.VMEM(coarse, F32),
            pltpu.VMEM(coarse, F32),
            pltpu.VMEM(coarse, F32),
            pltpu.VMEM(wide, BF16),
            pltpu.VMEM(wide, BF16),
            pltpu.VMEM(wide, BF16),
        ]
        + [pltpu.VMEM((channels, channels), F32)] * 3
        + sems(len(OUT))
        + sems(len(BACK))
        + sems(1)
        + sems(1)
        + [
            pltpu.SemaphoreType.DMA((chunks,)),
            pltpu.SemaphoreType.DMA,
            pltpu.SemaphoreType.DMA,
            pltpu.SemaphoreType.DMA((TABLES,)),
            pltpu.SemaphoreType.DMA((3,)),
        ],
        compiler_params=pltpu.CompilerParams(
            collective_id=0, has_side_effects=True, vmem_limit_bytes=48 * 1024 * 1024
        ),
        name="main",
    )(features, turned, middle_weights, *matrices, *tables)


def final_kernel(
    slab_ref, ty_hbm, tz_hbm, lifted_ref, proj_ref, base_ref, out_hbm,
    ty_ref, tz_ref, sum_ref, spec_ref, load_sem, save_sem,
):
    loads = [
        pltpu.make_async_copy(source, target, load_sem.at[i])
        for i, (source, target) in enumerate(
            ((ty_hbm, ty_ref), (tz_hbm, tz_ref))
        )
    ]
    for load in loads:
        load.start()
    for load in loads:
        load.wait()
    channels, half_y, _ = lifted_ref.shape
    local_x = base_ref.shape[1]
    modes = ty_ref.shape[1] // 3
    parts = tz_ref.shape[0] // (3 * 128)
    chunks = channels // CHUNK
    c_size = modes * parts
    stacked = []
    for h in range(chunks):
        wide = jnp.concatenate(
            [slab_ref[pl.ds(h * c_size + p, modes, stride=parts), :] for p in range(parts)], 1
        )
        stacked.append(dot_left3(ty_ref[...], wide))
    grown = jnp.concatenate(stacked, 0)
    high, low = split(grown)
    left = jnp.concatenate([high, low, high], 1)
    lane = lax.broadcasted_iota(jnp.int32, left.shape, 1) // (128 // CHUNK) % (CHUNK // 2)

    pairs = CHUNK // 2
    for c in range(pairs):
        done = dot(jnp.where(lane == c, left, jnp.zeros_like(left)), tz_ref[...])
        for h in range(chunks):
            for k in range(2):
                spec_ref[h * CHUNK + k * pairs + c] = done[
                    h * half_y : (h + 1) * half_y, k * 128 : (k + 1) * 128
                ]

    saves = []
    for g in range(half_y // 16):
        at = [pl.ds(g * 16 + 8 * k, 8) for k in range(2)]
        pooled = jnp.concatenate([lifted_ref[:, a, :].reshape(channels * 8, 128) for a in at], 1)
        spectral = jnp.concatenate([spec_ref[:, a, :].reshape(channels * 8, 128) for a in at], 1)
        added = dot_left3(proj_ref[...], gelu(pooled + spectral))
        for k in range(2):
            for b in range(2):
                piece = added[b * channels * 8 : (b + 1) * channels * 8, k * 128 : (k + 1) * 128]
                piece = piece.reshape(channels, 8, 128)
                rows = pl.ds(g * 32 + 16 * k + 8 * b, 8)
                for x in range(local_x):
                    sum_ref[:, x, rows, :] = base_ref[:, x, rows, :] + piece
            rows = pl.ds(g * 32 + 16 * k, 16)
            save = pltpu.make_async_copy(
                sum_ref.at[:, :, rows, :], out_hbm.at[:, :, rows, :], save_sem.at[2 * g + k]
            )
            save.start()
            saves.append(save)
    for save in saves:
        save.wait()


def on_device(features, fine_weights, middle_weights, lift_fine, lift_middle, project_out):
    channels, local_x, cells_y, cells_z = features.shape
    n = lax.axis_size("gx")
    owned = fine_weights.shape[0]
    owned_c = middle_weights.shape[0]
    half_ky, half_kz = KY // 2, KZ // 2
    narrow = 128 // CHUNK
    fits = (
        owned == 3 * KZ
        and KZ == 32
        and KY == 3 * n
        and n % 4 == 0
        and n & (n - 1) == 0
        and owned_c % narrow == 0
        and local_x == 2
        and cells_z == 128
        and cells_y % 32 == 0
        and channels == 3 * CHUNK
    )
    if not fits:
        return general_device(
            features, fine_weights, middle_weights, lift_fine, lift_middle, project_out
        )
    modes_x = fine_weights.shape[1]
    modes_c = middle_weights.shape[1]
    tx = np.asarray(host_table(modes_x, local_x * n), np.float32).reshape(modes_x, n, local_x)
    txc = np.asarray(host_table(modes_c, n), np.float32)

    half_y, half_z = cells_y // 2, cells_z // 2
    pool_y = np.repeat(np.eye(half_y), 2, axis=1) * 0.5
    pool_z = np.repeat(np.eye(half_z), 2, axis=1) * 0.25
    ty_c = host_table(half_ky, half_y)
    tz_c = host_table(half_kz, half_z)
    parts = half_kz // narrow
    chunks = channels // CHUNK
    ty = left_rows(host_table(KY, cells_y))
    tz = right_three(np.tile(host_table(KZ, cells_z).T, (1, 4)))
    yc = left_rows(np.concatenate([pool_y, ty_c @ pool_y], 0))
    zc_full = (tz_c @ pool_z).T.reshape(cells_z, parts, 1, narrow)
    zc = right_three(np.broadcast_to(zc_full, (cells_z, parts, CHUNK, narrow)).reshape(cells_z, -1))
    zp = np.repeat(pool_z, 2, axis=0).T
    zp = np.asarray(zp, jnp.bfloat16)
    zp = jnp.asarray(np.concatenate([zp, zp], 0))
    ty_i = left_three(host_table(KY, cells_y).T)
    tz_i = right_three(np.kron(np.eye(4), host_table(KZ, cells_z)))
    width = channels * narrow
    turn = np.zeros((width, 2 * width), np.float32)
    for c in range(channels):
        for j in range(narrow):
            turn[c * narrow + j, j * channels + c] = 1.0
            turn[c, width + c * narrow + j] = 1.0
            turn[channels + c, width + c * narrow + j] = 1.0
    turn = jnp.asarray(turn.astype(jnp.bfloat16))
    slab, lifted, base, projm = main_call(
        n, tx, txc, features, fine_weights, middle_weights,
        (lift_fine, lift_middle, project_out), (ty, tz, ty_i, tz_i, yc, zc, zp, turn),
    )

    tyc_i = left_three(ty_c.T)
    grown = np.zeros((parts, 2, CHUNK // 2, narrow, 2, cells_z))
    for k in range(2):
        grown[:, k, :, :, k] = np.repeat(tz_c, 2, axis=1).reshape(parts, 1, narrow, cells_z)
    tzc_i = right_three(grown.reshape(-1, 2 * cells_z))
    return pl.pallas_call(
        final_kernel,
        out_shape=jax.ShapeDtypeStruct(features.shape, F32),
        in_specs=[whole(), far(), far(), whole(), whole(), whole()],
        out_specs=far(),
        scratch_shapes=[
            pltpu.VMEM(tyc_i.shape, tyc_i.dtype),
            pltpu.VMEM(tzc_i.shape, tzc_i.dtype),
            pltpu.VMEM(features.shape, F32),
            pltpu.VMEM((channels, half_y, 128), F32),
            pltpu.SemaphoreType.DMA((2,)),
            pltpu.SemaphoreType.DMA((half_y // 8,)),
        ],
        compiler_params=pltpu.CompilerParams(vmem_limit_bytes=24 * 1024 * 1024),
        name="final",
    )(slab, tyc_i, tzc_i, lifted, projm, base)


def solution(mesh):
    in_specs = (
        P(None, ("groups", "gx"), None, None),
        P("gx", None, None, None),
        P("gx", None, None, None),
        P(),
        P(),
        P(),
    )
    out_specs = P(None, ("groups", "gx"), None, None)
    return jax.shard_map(
        on_device, mesh=mesh, in_specs=in_specs, out_specs=out_specs, check_vma=False
    )
```

```python
import functools

import jax
import jax.numpy as jnp
import numpy as np
from jax import lax
from jax.experimental import pallas as pl
from jax.experimental.pallas import tpu as pltpu
from jax.sharding import PartitionSpec as P

KY = 48
KZ = 32


HIGHEST = lax.Precision.HIGHEST


def cosine_table(modes_kept, length, columns):
    orders = jnp.arange(modes_kept, dtype=jnp.int32)[:, None]
    points = jnp.arange(columns, dtype=jnp.int32)[None, :]
    phase = orders * (2 * points + 1) % (4 * length)
    angle = jnp.pi / (2 * length) * phase.astype(jnp.float32)
    scales = jnp.where(
        orders == 0, jnp.sqrt(jnp.float32(1.0 / length)), jnp.sqrt(jnp.float32(2.0 / length))
    )
    return scales * jnp.cos(angle)


def forward_yz(values, modes_y, modes_z):
    channels, local_x, cells_y, cells_z = values.shape
    table_z = cosine_table(modes_z, cells_z, cells_z)
    table_y = cosine_table(modes_y, cells_y, cells_y)
    along_z = jnp.einsum("cxyz,jz->cxyj", values, table_z, precision=HIGHEST)
    both = jnp.einsum("cxyj,iy->ijxc", along_z, table_y, precision=HIGHEST)
    return both.reshape(modes_y * modes_z, local_x, channels)


def inverse_yz(coeffs, modes_y, modes_z, cells_y, cells_z):
    total, local_x, channels = coeffs.shape
    shaped = coeffs.reshape(modes_y, modes_z, local_x, channels)
    table_z = cosine_table(modes_z, cells_z, cells_z)
    table_y = cosine_table(modes_y, cells_y, cells_y)
    along_y = jnp.einsum("ijxc,iy->jxcy", shaped, table_y, precision=HIGHEST)
    return jnp.einsum("jxcy,jz->cxyz", along_y, table_z, precision=HIGHEST)


def mix_modes(modal, weights):
    return jnp.einsum(
        "mkc,mkco->mko", modal.astype(jnp.bfloat16), weights, preferred_element_type=jnp.float32
    )


def pointwise(values, matrix):
    return jnp.einsum("cxyz,co->oxyz", values, matrix, precision=HIGHEST)


def coarsen(values):
    channels, cells_x, cells_y, cells_z = values.shape
    shaped = values.reshape(channels, cells_x // 2, 2, cells_y // 2, 2, cells_z // 2, 2)
    return jnp.mean(shaped, axis=(2, 4, 6))


def refine(values):
    return jnp.repeat(jnp.repeat(jnp.repeat(values, 2, axis=1), 2, axis=2), 2, axis=3)


def general_device(features, fine_weights, middle_weights, lift_fine, lift_middle, project_out):
    channels, local_x, cells_y, cells_z = features.shape
    group_size = lax.axis_size("gx")
    cells_x = local_x * group_size
    modes_x = fine_weights.shape[1]
    coeffs = forward_yz(features, KY, KZ)
    table_x = cosine_table(modes_x, cells_x, cells_x)
    owned_pairs = coeffs.shape[0] // group_size
    grouped = coeffs.reshape(group_size, owned_pairs, local_x, channels)
    modal = jnp.einsum(
        "amxc,kx->mkc",
        lax.all_to_all(grouped, "gx", split_axis=0, concat_axis=2, tiled=True),
        table_x,
        precision=HIGHEST,
    )
    mixed = mix_modes(modal, fine_weights)
    back = jnp.einsum("mkc,kx->mxc", mixed, table_x, precision=HIGHEST)
    slabs = lax.all_to_all(back, "gx", split_axis=1, concat_axis=0, tiled=True)
    level_one = jax.nn.gelu(
        inverse_yz(slabs, KY, KZ, cells_y, cells_z) + pointwise(features, lift_fine),
        approximate=False,
    )
    pooled = coarsen(level_one)
    half_x = local_x // 2
    half_ky = KY // 2
    half_kz = KZ // 2
    half_modes = middle_weights.shape[1]
    coarse_x = half_x * group_size
    coarse_coeffs = forward_yz(pooled, half_ky, half_kz)
    coarse_pencils = lax.all_to_all(coarse_coeffs, "gx", split_axis=0, concat_axis=1, tiled=True)
    coarse_table = cosine_table(half_modes, coarse_x, coarse_x)
    coarse_modal = jnp.einsum("mxc,kx->mkc", coarse_pencils, coarse_table, precision=HIGHEST)
    coarse_mixed = mix_modes(coarse_modal, middle_weights)
    coarse_back = jnp.einsum("mkc,kx->mxc", coarse_mixed, coarse_table, precision=HIGHEST)
    coarse_slabs = lax.all_to_all(coarse_back, "gx", split_axis=1, concat_axis=0, tiled=True)
    level_two = jax.nn.gelu(
        inverse_yz(coarse_slabs, half_ky, half_kz, cells_y // 2, cells_z // 2)
        + pointwise(pooled, lift_middle),
        approximate=False,
    )
    return features + pointwise(level_one + refine(level_two), project_out)


BF16 = jnp.bfloat16
MESH = pl.DeviceIdType.MESH
F32 = jnp.float32


def host_table(modes_kept, length):
    orders = np.arange(modes_kept)[:, None]
    points = np.arange(length)[None, :]
    scales = np.where(orders == 0, np.sqrt(1.0 / length), np.sqrt(2.0 / length))
    return scales * np.cos(np.pi * orders * (2 * points + 1) / (2 * length))


def host_split(table):
    table = np.asarray(table, np.float32)
    high = table.astype(jnp.bfloat16)
    low = (table - high.astype(np.float32)).astype(jnp.bfloat16)
    return high, low


def left_rows(table):
    high, low = host_split(table)
    return jnp.asarray(
        np.concatenate([np.concatenate([high, high], 1), np.concatenate([low, low], 1)], 0)
    )


def left_three(table):
    high, low = host_split(table)
    return jnp.asarray(np.concatenate([high, high, low], 1))


def right_three(table):
    high, low = host_split(table)
    return jnp.asarray(np.concatenate([high, high, low], 0))


def split(values):
    high = values.astype(BF16)
    low = (values - high.astype(F32)).astype(BF16)
    return high, low


def dot(left, right):
    return jnp.dot(left, right, preferred_element_type=F32)


def dot_left3(left3, values):
    high, low = split(values)
    return dot(left3, jnp.concatenate([high, low, high], 0))


def dot_right3(values, right3):
    high, low = split(values)
    return dot(jnp.concatenate([high, low, high], 1), right3)


def gelu(t):
    return 0.5 * t * (1.0 + lax.erf(t * np.float32(np.sqrt(0.5))))


def far():
    return pl.BlockSpec(memory_space=pl.ANY)


def whole():
    return pl.BlockSpec(memory_space=pltpu.VMEM)


def widen(matrix_ref, targets):
    channels = matrix_ref.shape[0]
    size = channels * 8
    row = lax.broadcasted_iota(jnp.int32, (size, channels), 0) // 8
    pick = (row == lax.broadcasted_iota(jnp.int32, (size, channels), 1)).astype(F32).astype(BF16)
    col = lax.broadcasted_iota(jnp.int32, (channels, size), 1) // 8
    place = (col == lax.broadcasted_iota(jnp.int32, (channels, size), 0)).astype(F32).astype(BF16)
    left = lax.broadcasted_iota(jnp.int32, (size, size), 0) % 8
    right = lax.broadcasted_iota(jnp.int32, (size, size), 1) % 8
    for part, spots in zip(split(matrix_ref[...]), ((0, 1), (2,))):
        grown = lax.dot_general(pick, part, (((1,), (1,)), ((), ())), preferred_element_type=F32)
        grown = dot(grown.astype(BF16), place)
        for ref, at, rule in targets:
            value = jnp.where(rule(left, right), grown, 0.0).astype(BF16)
            for spot in spots:
                ref[at : at + size, spot * size : (spot + 1) * size] = value


def same(left, right):
    return left == right


def load_block(ref, at):
    channels, local_x, _, cells_z = ref.shape
    return jnp.concatenate([ref[:, x, at, :].reshape(channels * 8, cells_z) for x in range(local_x)], 1)


def store_block(ref, at, value):
    channels, local_x, _, cells_z = ref.shape
    for x in range(local_x):
        ref[:, x, at, :] = value[:, x * cells_z : (x + 1) * cells_z].reshape(channels, 8, cells_z)


def greet(n):
    me = lax.axis_index("gx")
    barrier = pltpu.get_barrier_semaphore()
    for d in range(1, n):
        pl.semaphore_signal(barrier, 1, device_id={"gx": lax.rem(me + d, n)}, device_id_type=MESH)
    pl.semaphore_wait(barrier, n - 1)


class Exchange:
    def __init__(self, n, parts, source, target, send_sem, recv_sem, own_sem):
        self.n, self.parts, self.source, self.target = n, parts, source, target
        self.send_sem, self.recv_sem, self.own_sem = send_sem, recv_sem, own_sem
        self.me = lax.axis_index("gx")

    def copy(self, part, d):
        peer = jnp.bitwise_xor(self.me, d)
        rows = pl.ds(*self.parts[part])
        return pltpu.make_async_remote_copy(
            src_ref=self.source.at[peer, rows],
            dst_ref=self.target.at[self.me, rows],
            send_sem=self.send_sem.at[part, d],
            recv_sem=self.recv_sem.at[part, d],
            device_id={"gx": peer},
            device_id_type=MESH,
        )

    def own(self, part):
        rows = pl.ds(*self.parts[part])
        return pltpu.make_async_copy(
            self.source.at[self.me, rows], self.target.at[self.me, rows], self.own_sem.at[part]
        )

    def start(self, part):
        for d in range(self.n - 1, 0, -1):
            self.copy(part, d).start()
        self.own(part).start()

    def wait(self, part):
        for d in range(1, self.n):
            self.copy(part, d).wait()
        self.own(part).wait()

    def after(self, q, action):
        for part, chunks in enumerate(self.chunks):
            last = chunks[-1] if action == self.start else chunks[0]
            pl.when(q == last)(functools.partial(action, part))


OUT = ((0,), (1, 2))
BACK = ((0,), (1,), (2,))


def chunk_exchange(n, plan, *refs):
    rows = 3 * CHUNK // 2
    parts = [(chunks[0] * rows, len(chunks) * rows) for chunks in plan]
    exchange = Exchange(n, parts, *refs)
    exchange.chunks = plan
    return exchange


CHUNK = 16
TABLES = 8


def main_kernel(n, tx, txc, *refs):
    refs = list(refs)
    f_hbm, w_hbm, wm_hbm = refs[:3]
    matrix_hbm = refs[3:6]
    table_hbm = refs[6 : 6 + TABLES]
    slab_ref, lifted_ref, base_ref, final_wide = refs[6 + TABLES : 10 + TABLES]
    rest = refs[10 + TABLES :]
    tables = rest[:TABLES]
    (
        f_ref, w_ref, wm_ref, lev_ref, grown_ref, wire_one, got_one, wire_two, got_two,
        modal, mixed, flat_ref, modes_ref, pooled_ref, coarse_ref, stage, got_three, back_c, got_four,
        lift_wide, middle_wide, proj_wide, lift_ref, middle_ref, project_ref,
        send_one, recv_one, own_one, send_two, recv_two, own_two,
        send_three, recv_three, own_three, send_four, recv_four, own_four,
        f_sem, w_sem, wm_sem, table_sem, matrix_sem,
    ) = rest[TABLES:]
    ty_ref, tz_ref, tyi_ref, tzi_ref, yc_ref, zc_ref, zp_ref, perm_ref = tables
    channels, local_x, cells_y, cells_z = f_ref.shape
    modes_x, _, _, owned = w_ref.shape
    modes_y = ty_ref.shape[0] // 2
    per = modes_y // n
    chunks = channels // CHUNK
    rows = local_x * CHUNK
    half = CHUNK // 2
    quad = 4
    size_q = 3 * half

    def at_chunk(q):
        return pl.ds(pl.multiple_of(q * size_q, 8), size_q)

    me = lax.axis_index("gx")
    barrier = pltpu.get_barrier_semaphore()
    for d in range(n - 1, 0, -1):
        pl.semaphore_signal(
            barrier, 1, device_id={"gx": jnp.bitwise_xor(me, d)}, device_id_type=MESH
        )

    loads = [
        pltpu.make_async_copy(
            f_hbm.at[pl.ds(q * CHUNK, CHUNK)], f_ref.at[pl.ds(q * CHUNK, CHUNK)], f_sem.at[q]
        )
        for q in range(chunks)
    ]
    fills = [
        pltpu.make_async_copy(source, target, table_sem.at[i])
        for i, (source, target) in enumerate(zip(table_hbm, tables))
    ]
    fills += [
        pltpu.make_async_copy(source, target, matrix_sem.at[i])
        for i, (source, target) in enumerate(
            zip(matrix_hbm, (lift_ref, middle_ref, project_ref))
        )
    ]
    loads[0].start()
    fills[0].start()
    fills[1].start()
    for load in loads[1:]:
        load.start()
    for fill in fills[2:]:
        fill.start()
    fetch = pltpu.make_async_copy(w_hbm, w_ref, w_sem)
    fetch_c = pltpu.make_async_copy(wm_hbm, wm_ref, wm_sem)

    one = chunk_exchange(n, OUT, wire_one, got_one, send_one, recv_one, own_one)
    two = chunk_exchange(n, BACK, wire_two, got_two, send_two, recv_two, own_two)
    small = [(0, stage.shape[1])]
    three = Exchange(n, small, stage, got_three, send_three, recv_three, own_three)
    four = Exchange(n, small, back_c, got_four, send_four, recv_four, own_four)

    fills[0].wait()
    fills[1].wait()
    tail_lane = lax.broadcasted_iota(jnp.int32, (3 * half, 128), 1) // 32

    def forward(q, carry):
        pltpu.make_async_copy(
            f_hbm.at[pl.ds(q * CHUNK, CHUNK)], f_ref.at[pl.ds(q * CHUNK, CHUNK)], f_sem.at[q]
        ).wait()

        def channel(c, inner):
            wide = jnp.concatenate([f_ref[q * CHUNK + c, x] for x in range(local_x)], 1)
            high, low = split(wide)
            both = dot(ty_ref[...], jnp.concatenate([high, low], 0))
            both = both[:modes_y] + both[modes_y:]
            for x in range(local_x):
                grown_ref[pl.ds(x * CHUNK + c, modes_y, stride=rows), :] = both[
                    :, x * cells_z : (x + 1) * cells_z
                ]
            return inner

        lax.fori_loop(0, CHUNK, channel, 0, unroll=8)

        def owners(b, inner):
            size = quad * per * rows
            done = dot_right3(grown_ref[pl.ds(pl.multiple_of(b * size, 8), size), :], tz_ref[...])
            for k in range(quad):
                part = done[k * per * rows : (k + 1) * per * rows]
                total = jnp.concatenate(
                    [part[g * rows + 3 * half : (g + 1) * rows] for g in range(per)], 0
                )
                for g in range(per):
                    total = jnp.where(tail_lane == g, part[g * rows : g * rows + 3 * half], total)
                wire_one[b * quad + k, at_chunk(q)] = total
            return inner

        lax.fori_loop(0, n // quad, owners, 0, unroll=2)

        @pl.when(q == 0)
        def _():
            pl.semaphore_wait(barrier, n - 1)

        one.after(q, one.start)
        return carry

    lax.fori_loop(0, chunks, forward, 0)
    fetch.start()
    fetch_c.start()

    for fill in fills[2:]:
        fill.wait()
    widen(lift_ref, ((lift_wide, 0, same),))

    def lift(b, carry):
        at = pl.ds(pl.multiple_of(b * 8, 8), 8)
        store_block(lev_ref, at, dot_left3(lift_wide[...], load_block(f_ref, at)))
        return carry

    lax.fori_loop(0, cells_y // 8, lift, 0)
    mixed[...] = jnp.zeros_like(mixed)
    fetch.wait()
    fetch_c.wait()

    small_lane = lax.broadcasted_iota(jnp.int32, (half, 128), 1) // 32

    def absorb(q, carry):
        one.after(q, one.wait)
        for k in range(modes_x):
            first = sum(got_one[a, pl.ds(pl.multiple_of(q * size_q, 8), CHUNK)] * np.float32(tx[k, a, 0]) for a in range(n))
            second = sum(got_one[a, at_chunk(q)] * np.float32(tx[k, a, 1]) for a in range(n))
            extra = jnp.zeros((half, 128), F32)
            for g in range(3):
                piece = pltpu.roll(second[g * half : (g + 1) * half], 32 * (g + 1), 1)
                extra = jnp.where(small_lane == g, piece, extra)
            total = first + jnp.concatenate([second[CHUNK:], extra], 0)
            modal[k, pl.ds(pl.multiple_of(q * CHUNK, 8), CHUNK)] = total.astype(BF16).astype(F32)

        @pl.when(q < chunks - 1)
        def _():
            def mode(k, inner):
                total = mixed[k, :, :owned]
                for c in range(CHUNK):
                    at = q * CHUNK + c
                    total += modal[k, pl.ds(at, 1), :owned] * w_ref[k, at].astype(F32)
                mixed[k, :, :owned] = total
                return inner

            lax.fori_loop(0, modes_x, mode, 0, unroll=2)

        return carry

    lax.fori_loop(0, chunks, absorb, 0)

    wide_lane = lax.broadcasted_iota(jnp.int32, (3 * half, 128), 1)

    def back(h, carry):
        at = pl.ds(pl.multiple_of(h * CHUNK, CHUNK), CHUNK)

        def mode(k, inner):
            total = mixed[k, at, :owned]
            for c in range(channels - CHUNK, channels):
                total += modal[k, c : c + 1, :owned] * w_ref[k, c, at].astype(F32)
            mixed[k, at, :owned] = total
            return inner

        lax.fori_loop(0, modes_x, mode, 0, unroll=2)
        value = [mixed[k, at] for k in range(modes_x)]
        for a in range(n):
            first = sum(value[k] * np.float32(tx[k, a, 0]) for k in range(modes_x))
            second = sum(value[k] * np.float32(tx[k, a, 1]) for k in range(modes_x))
            rolled = jnp.concatenate(
                [pltpu.roll(second[half:], 96 - 32 * g, 1) for g in range(3)], 0
            )
            wire_two[a, at_chunk(h)] = jnp.where(
                wide_lane < 96, jnp.concatenate([first, second[:half]], 0), rolled
            )
        two.after(h, two.start)
        return carry

    lax.fori_loop(0, chunks, back, 0)

    size = channels * 8
    widen(middle_ref, ((middle_wide, 0, same),))
    widen(
        project_ref,
        (
            (proj_wide, 0, same),
            (final_wide, 0, lambda left, right: left // 2 == right),
            (final_wide, size, lambda left, right: left // 2 + 4 == right),
        ),
    )

    half_y = cells_y // 2
    modes_c = yc_ref.shape[0] // 2 - half_y
    parts = zc_ref.shape[1] // 128
    narrow = 128 // CHUNK
    coarse_lane = (
        lax.broadcasted_iota(jnp.int32, (modes_c, parts * 128), 1) // narrow % CHUNK
    )
    c_rows = modes_c + half_y

    def middle(h, carry):
        two.after(h, two.wait)

        values = [got_two[a, at_chunk(h)] for a in range(n)]
        done = dot_right3(jnp.concatenate(values, 0), tzi_ref[...])
        for a in range(n):
            part = done[a * size_q : (a + 1) * size_q]
            for g in range(per):
                at = (a * per + g) * rows
                grown_ref[at : at + size_q] = part[:, g * 128 : (g + 1) * 128]
                grown_ref[at + size_q : at + rows] = part[g * half : (g + 1) * half, per * 128 :]

        def level(pair, inner):
            sums = []
            for o in range(2):
                o = 2 * pair + o
                wide = jnp.concatenate(
                    [grown_ref[pl.ds(x * CHUNK + o, modes_y, stride=rows), :] for x in range(local_x)],
                    1,
                )
                done = dot_left3(tyi_ref[...], wide)
                at = h * CHUNK + o
                values = []
                for x in range(local_x):
                    value = gelu(lev_ref[at, x] + done[:, x * cells_z : (x + 1) * cells_z])
                    lev_ref[at, x] = value
                    values.append(value)
                sums.append(values[0] + values[1])
            high, low = split(jnp.concatenate(sums, 1))
            both = dot(yc_ref[...], jnp.concatenate([high, low], 0))
            both = both[:c_rows] + both[c_rows:]
            for o in range(2):
                part = both[:, o * 128 : (o + 1) * 128]
                o = 2 * pair + o
                flat_ref[h * CHUNK + o] = part[:half_y]
                modes_ref[pl.ds(pl.multiple_of(o * modes_c, 8), modes_c), :] = part[half_y:]
            return inner

        lax.fori_loop(0, CHUNK // 2, level, 0, unroll=8)

        done = dot_right3(modes_ref[...], zc_ref[...])
        total = jnp.zeros((modes_c, parts * 128), F32)
        for o in range(CHUNK):
            total = jnp.where(coarse_lane == o, done[o * modes_c : (o + 1) * modes_c], total)
        for p in range(parts):
            coarse_ref[pl.ds(h * modes_c * parts + p, modes_c, stride=parts), :] = total[
                :, p * 128 : (p + 1) * 128
            ]
        return carry

    lax.fori_loop(0, chunks, middle, 0)

    count = stage.shape[1]
    c_size = modes_c * parts
    for a in range(n):
        for h in range(chunks):
            stage[a, :, h * 128 : (h + 1) * 128] = coarse_ref[
                h * c_size + a * count : h * c_size + (a + 1) * count
            ]
    three.start(0)

    def project(b, carry):
        at = pl.ds(pl.multiple_of(b * 8, 8), 8)
        done = dot_left3(proj_wide[...], load_block(lev_ref, at))
        store_block(base_ref, at, load_block(f_ref, at) + done)
        return carry

    def pool(h, carry):
        at = pl.ds(h * CHUNK, CHUNK)
        high, low = split(flat_ref[at].reshape(CHUNK * half_y, 128))
        mean = dot(jnp.concatenate([high, low], 1), zp_ref[...])
        pooled_ref[at] = mean.reshape(CHUNK, half_y, 128)
        return carry

    lax.fori_loop(0, chunks, pool, 0)
    blocks = cells_y // 8
    lax.fori_loop(0, blocks // 2, project, 0, unroll=3)
    three.wait(0)
    modes_k = wm_ref.shape[1]
    wave = [
        sum(got_three[a] * np.float32(txc[k, a]) for a in range(n)) for k in range(modes_k)
    ]
    wave = jnp.concatenate(wave, 0).astype(BF16)
    turned = dot(wave, perm_ref[:, : wave.shape[1]])
    width = wave.shape[1]
    keep = (
        lax.broadcasted_iota(jnp.int32, (narrow, width), 1) // channels
        == lax.broadcasted_iota(jnp.int32, (narrow, width), 0)
    )
    outs = []
    for k in range(modes_k):
        for t in range(count):
            row = turned[k * count + t : k * count + t + 1]
            left = jnp.where(keep, jnp.broadcast_to(row, (narrow, width)), 0.0).astype(BF16)
            right = wm_ref[t * narrow : (t + 1) * narrow, k].reshape(narrow * channels, channels)
            outs.append(dot(left, right))
    high, low = split(jnp.concatenate(outs, 0))
    spread = perm_ref[: 2 * channels, width:]
    grown = dot(jnp.concatenate([high, low], 1), spread)
    ours = (
        lax.broadcasted_iota(jnp.int32, grown.shape, 1) % narrow
        == lax.broadcasted_iota(jnp.int32, grown.shape, 0) % narrow
    )
    grown = jnp.where(ours, grown, 0.0).reshape(modes_k * count, narrow, width).sum(1)
    for a in range(n):
        back_c[a] = sum(
            grown[k * count : (k + 1) * count] * np.float32(txc[k, a]) for k in range(modes_k)
        )
    four.start(0)

    def lift_coarse(g, carry):
        at = [pl.ds(pl.multiple_of(g * 16 + 8 * k, 8), 8) for k in range(2)]
        pooled = jnp.concatenate([pooled_ref[:, a, :].reshape(channels * 8, 128) for a in at], 1)
        done = dot_left3(middle_wide[...], pooled)
        for k in range(2):
            lifted_ref[:, at[k], :] = done[:, k * 128 : (k + 1) * 128].reshape(channels, 8, 128)
        return carry

    lax.fori_loop(0, half_y // 16, lift_coarse, 0)
    lax.fori_loop(blocks // 2, blocks, project, 0, unroll=3)
    four.wait(0)
    for a in range(n):
        for h in range(chunks):
            slab_ref[h * c_size + a * count : h * c_size + (a + 1) * count, :] = got_four[
                a, :, h * 128 : (h + 1) * 128
            ]


def main_call(n, tx, txc, features, weights, middle_weights, matrices, tables):
    channels, local_x, cells_y, cells_z = features.shape
    turned = jnp.transpose(weights, (1, 2, 3, 0))
    modes_x = turned.shape[0]
    size = channels * 8
    chunks = channels // CHUNK
    wire = (n, chunks * 3 * CHUNK // 2, 128)
    c_rows = (KY // 2) * (KZ // 2) // (128 // CHUNK)
    coarse = (n, c_rows // n, channels * 128 // CHUNK)
    wide = (size, 3 * size)

    def sems(slots):
        return [
            pltpu.SemaphoreType.DMA((slots, n)),
            pltpu.SemaphoreType.DMA((slots, n)),
            pltpu.SemaphoreType.DMA((slots,)),
        ]

    return pl.pallas_call(
        functools.partial(main_kernel, n, tx, txc),
        out_shape=(
            pltpu.VMEM((c_rows * chunks, 128), F32),
            pltpu.VMEM((channels, cells_y // 2, 128), F32),
            pltpu.VMEM(features.shape, F32),
            pltpu.VMEM((2 * size, 3 * size), BF16),
        ),
        in_specs=[far()] * (6 + TABLES),
        out_specs=(whole(),) * 4,
        scratch_shapes=[pltpu.VMEM(table.shape, table.dtype) for table in tables]
        + [
            pltpu.VMEM(features.shape, F32),
            pltpu.VMEM(turned.shape, BF16),
            pltpu.VMEM(middle_weights.shape, BF16),
            pltpu.VMEM(features.shape, F32),
            pltpu.VMEM((KY * local_x * CHUNK, cells_z), F32),
            pltpu.VMEM(wire, F32),
            pltpu.VMEM(wire, F32),
            pltpu.VMEM(wire, F32),
            pltpu.VMEM(wire, F32),
            pltpu.VMEM((modes_x, channels, 128), F32),
            pltpu.VMEM((modes_x, channels, 128), F32),
            pltpu.VMEM((channels, cells_y // 2, 128), F32),
            pltpu.VMEM((CHUNK * KY // 2, 128), F32),
            pltpu.VMEM((channels, cells_y // 2, 128), F32),
            pltpu.VMEM((c_rows * chunks, 128), F32),
            pltpu.VMEM(coarse, F32),
            pltpu.VMEM(coarse, F32),
            pltpu.VMEM(coarse, F32),
            pltpu.VMEM(coarse, F32),
            pltpu.VMEM(wide, BF16),
            pltpu.VMEM(wide, BF16),
            pltpu.VMEM(wide, BF16),
        ]
        + [pltpu.VMEM((channels, channels), F32)] * 3
        + sems(len(OUT))
        + sems(len(BACK))
        + sems(1)
        + sems(1)
        + [
            pltpu.SemaphoreType.DMA((chunks,)),
            pltpu.SemaphoreType.DMA,
            pltpu.SemaphoreType.DMA,
            pltpu.SemaphoreType.DMA((TABLES,)),
            pltpu.SemaphoreType.DMA((3,)),
        ],
        compiler_params=pltpu.CompilerParams(
            collective_id=0, has_side_effects=True, vmem_limit_bytes=48 * 1024 * 1024
        ),
        name="main",
    )(features, turned, middle_weights, *matrices, *tables)


def final_kernel(
    slab_ref, ty_hbm, tz_hbm, lifted_ref, proj_ref, base_ref, out_hbm,
    ty_ref, tz_ref, sum_ref, spec_ref, load_sem, save_sem,
):
    loads = [
        pltpu.make_async_copy(source, target, load_sem.at[i])
        for i, (source, target) in enumerate(
            ((ty_hbm, ty_ref), (tz_hbm, tz_ref))
        )
    ]
    for load in loads:
        load.start()
    for load in loads:
        load.wait()
    channels, half_y, _ = lifted_ref.shape
    local_x = base_ref.shape[1]
    modes = ty_ref.shape[1] // 3
    parts = tz_ref.shape[0] // (3 * 128)
    chunks = channels // CHUNK
    c_size = modes * parts
    stacked = []
    for h in range(chunks):
        wide = jnp.concatenate(
            [slab_ref[pl.ds(h * c_size + p, modes, stride=parts), :] for p in range(parts)], 1
        )
        stacked.append(dot_left3(ty_ref[...], wide))
    grown = jnp.concatenate(stacked, 0)
    high, low = split(grown)
    left = jnp.concatenate([high, low, high], 1)
    lane = lax.broadcasted_iota(jnp.int32, left.shape, 1) // (128 // CHUNK) % (CHUNK // 2)

    pairs = CHUNK // 2
    for c in range(pairs):
        done = dot(jnp.where(lane == c, left, jnp.zeros_like(left)), tz_ref[...])
        for h in range(chunks):
            for k in range(2):
                spec_ref[h * CHUNK + k * pairs + c] = done[
                    h * half_y : (h + 1) * half_y, k * 128 : (k + 1) * 128
                ]

    saves = []
    for g in range(half_y // 16):
        at = [pl.ds(g * 16 + 8 * k, 8) for k in range(2)]
        pooled = jnp.concatenate([lifted_ref[:, a, :].reshape(channels * 8, 128) for a in at], 1)
        spectral = jnp.concatenate([spec_ref[:, a, :].reshape(channels * 8, 128) for a in at], 1)
        added = dot_left3(proj_ref[...], gelu(pooled + spectral))
        for k in range(2):
            for b in range(2):
                piece = added[b * channels * 8 : (b + 1) * channels * 8, k * 128 : (k + 1) * 128]
                piece = piece.reshape(channels, 8, 128)
                rows = pl.ds(g * 32 + 16 * k + 8 * b, 8)
                for x in range(local_x):
                    sum_ref[:, x, rows, :] = base_ref[:, x, rows, :] + piece
            rows = pl.ds(g * 32 + 16 * k, 16)
            save = pltpu.make_async_copy(
                sum_ref.at[:, :, rows, :], out_hbm.at[:, :, rows, :], save_sem.at[2 * g + k]
            )
            save.start()
            saves.append(save)
    for save in saves:
        save.wait()


def on_device(features, fine_weights, middle_weights, lift_fine, lift_middle, project_out):
    channels, local_x, cells_y, cells_z = features.shape
    n = lax.axis_size("gx")
    owned = fine_weights.shape[0]
    owned_c = middle_weights.shape[0]
    half_ky, half_kz = KY // 2, KZ // 2
    narrow = 128 // CHUNK
    fits = (
        owned == 3 * KZ
        and KZ == 32
        and KY == 3 * n
        and n % 4 == 0
        and n & (n - 1) == 0
        and owned_c % narrow == 0
        and local_x == 2
        and cells_z == 128
        and cells_y % 32 == 0
        and channels == 3 * CHUNK
    )
    if not fits:
        return general_device(
            features, fine_weights, middle_weights, lift_fine, lift_middle, project_out
        )
    modes_x = fine_weights.shape[1]
    modes_c = middle_weights.shape[1]
    tx = np.asarray(host_table(modes_x, local_x * n), np.float32).reshape(modes_x, n, local_x)
    txc = np.asarray(host_table(modes_c, n), np.float32)

    half_y, half_z = cells_y // 2, cells_z // 2
    pool_y = np.repeat(np.eye(half_y), 2, axis=1) * 0.5
    pool_z = np.repeat(np.eye(half_z), 2, axis=1) * 0.25
    ty_c = host_table(half_ky, half_y)
    tz_c = host_table(half_kz, half_z)
    parts = half_kz // narrow
    chunks = channels // CHUNK
    ty = left_rows(host_table(KY, cells_y))
    tz = right_three(np.tile(host_table(KZ, cells_z).T, (1, 4)))
    yc = left_rows(np.concatenate([pool_y, ty_c @ pool_y], 0))
    zc_full = (tz_c @ pool_z).T.reshape(cells_z, parts, 1, narrow)
    zc = right_three(np.broadcast_to(zc_full, (cells_z, parts, CHUNK, narrow)).reshape(cells_z, -1))
    zp = np.repeat(pool_z, 2, axis=0).T
    zp = np.asarray(zp, jnp.bfloat16)
    zp = jnp.asarray(np.concatenate([zp, zp], 0))
    ty_i = left_three(host_table(KY, cells_y).T)
    tz_i = right_three(np.kron(np.eye(4), host_table(KZ, cells_z)))
    width = channels * narrow
    turn = np.zeros((width, 2 * width), np.float32)
    for c in range(channels):
        for j in range(narrow):
            turn[c * narrow + j, j * channels + c] = 1.0
            turn[c, width + c * narrow + j] = 1.0
            turn[channels + c, width + c * narrow + j] = 1.0
    turn = jnp.asarray(turn.astype(jnp.bfloat16))
    slab, lifted, base, projm = main_call(
        n, tx, txc, features, fine_weights, middle_weights,
        (lift_fine, lift_middle, project_out), (ty, tz, ty_i, tz_i, yc, zc, zp, turn),
    )

    tyc_i = left_three(ty_c.T)
    grown = np.zeros((parts, 2, CHUNK // 2, narrow, 2, cells_z))
    for k in range(2):
        grown[:, k, :, :, k] = np.repeat(tz_c, 2, axis=1).reshape(parts, 1, narrow, cells_z)
    tzc_i = right_three(grown.reshape(-1, 2 * cells_z))
    return pl.pallas_call(
        final_kernel,
        out_shape=jax.ShapeDtypeStruct(features.shape, F32),
        in_specs=[whole(), far(), far(), whole(), whole(), whole()],
        out_specs=far(),
        scratch_shapes=[
            pltpu.VMEM(tyc_i.shape, tyc_i.dtype),
            pltpu.VMEM(tzc_i.shape, tzc_i.dtype),
            pltpu.VMEM(features.shape, F32),
            pltpu.VMEM((channels, half_y, 128), F32),
            pltpu.SemaphoreType.DMA((2,)),
            pltpu.SemaphoreType.DMA((half_y // 8,)),
        ],
        compiler_params=pltpu.CompilerParams(vmem_limit_bytes=24 * 1024 * 1024),
        name="final",
    )(slab, tyc_i, tzc_i, lifted, projm, base)


def solution(mesh):
    in_specs = (
        P(None, ("groups", "gx"), None, None),
        P("gx", None, None, None),
        P("gx", None, None, None),
        P(),
        P(),
        P(),
    )
    out_specs = P(None, ("groups", "gx"), None, None)
    return jax.shard_map(
        on_device, mesh=mesh, in_specs=in_specs, out_specs=out_specs, check_vma=False
    )
```

```python
import functools

import jax
import jax.numpy as jnp
import numpy as np
from jax import lax
from jax.experimental import pallas as pl
from jax.experimental.pallas import tpu as pltpu
from jax.sharding import PartitionSpec as P

KY = 48
KZ = 32


HIGHEST = lax.Precision.HIGHEST


def cosine_table(modes_kept, length, columns):
    orders = jnp.arange(modes_kept, dtype=jnp.int32)[:, None]
    points = jnp.arange(columns, dtype=jnp.int32)[None, :]
    phase = orders * (2 * points + 1) % (4 * length)
    angle = jnp.pi / (2 * length) * phase.astype(jnp.float32)
    scales = jnp.where(
        orders == 0, jnp.sqrt(jnp.float32(1.0 / length)), jnp.sqrt(jnp.float32(2.0 / length))
    )
    return scales * jnp.cos(angle)


def forward_yz(values, modes_y, modes_z):
    channels, local_x, cells_y, cells_z = values.shape
    table_z = cosine_table(modes_z, cells_z, cells_z)
    table_y = cosine_table(modes_y, cells_y, cells_y)
    along_z = jnp.einsum("cxyz,jz->cxyj", values, table_z, precision=HIGHEST)
    both = jnp.einsum("cxyj,iy->ijxc", along_z, table_y, precision=HIGHEST)
    return both.reshape(modes_y * modes_z, local_x, channels)


def inverse_yz(coeffs, modes_y, modes_z, cells_y, cells_z):
    total, local_x, channels = coeffs.shape
    shaped = coeffs.reshape(modes_y, modes_z, local_x, channels)
    table_z = cosine_table(modes_z, cells_z, cells_z)
    table_y = cosine_table(modes_y, cells_y, cells_y)
    along_y = jnp.einsum("ijxc,iy->jxcy", shaped, table_y, precision=HIGHEST)
    return jnp.einsum("jxcy,jz->cxyz", along_y, table_z, precision=HIGHEST)


def mix_modes(modal, weights):
    return jnp.einsum(
        "mkc,mkco->mko", modal.astype(jnp.bfloat16), weights, preferred_element_type=jnp.float32
    )


def pointwise(values, matrix):
    return jnp.einsum("cxyz,co->oxyz", values, matrix, precision=HIGHEST)


def coarsen(values):
    channels, cells_x, cells_y, cells_z = values.shape
    shaped = values.reshape(channels, cells_x // 2, 2, cells_y // 2, 2, cells_z // 2, 2)
    return jnp.mean(shaped, axis=(2, 4, 6))


def refine(values):
    return jnp.repeat(jnp.repeat(jnp.repeat(values, 2, axis=1), 2, axis=2), 2, axis=3)


def general_device(features, fine_weights, middle_weights, lift_fine, lift_middle, project_out):
    channels, local_x, cells_y, cells_z = features.shape
    group_size = lax.axis_size("gx")
    cells_x = local_x * group_size
    modes_x = fine_weights.shape[1]
    coeffs = forward_yz(features, KY, KZ)
    table_x = cosine_table(modes_x, cells_x, cells_x)
    owned_pairs = coeffs.shape[0] // group_size
    grouped = coeffs.reshape(group_size, owned_pairs, local_x, channels)
    modal = jnp.einsum(
        "amxc,kx->mkc",
        lax.all_to_all(grouped, "gx", split_axis=0, concat_axis=2, tiled=True),
        table_x,
        precision=HIGHEST,
    )
    mixed = mix_modes(modal, fine_weights)
    back = jnp.einsum("mkc,kx->mxc", mixed, table_x, precision=HIGHEST)
    slabs = lax.all_to_all(back, "gx", split_axis=1, concat_axis=0, tiled=True)
    level_one = jax.nn.gelu(
        inverse_yz(slabs, KY, KZ, cells_y, cells_z) + pointwise(features, lift_fine),
        approximate=False,
    )
    pooled = coarsen(level_one)
    half_x = local_x // 2
    half_ky = KY // 2
    half_kz = KZ // 2
    half_modes = middle_weights.shape[1]
    coarse_x = half_x * group_size
    coarse_coeffs = forward_yz(pooled, half_ky, half_kz)
    coarse_pencils = lax.all_to_all(coarse_coeffs, "gx", split_axis=0, concat_axis=1, tiled=True)
    coarse_table = cosine_table(half_modes, coarse_x, coarse_x)
    coarse_modal = jnp.einsum("mxc,kx->mkc", coarse_pencils, coarse_table, precision=HIGHEST)
    coarse_mixed = mix_modes(coarse_modal, middle_weights)
    coarse_back = jnp.einsum("mkc,kx->mxc", coarse_mixed, coarse_table, precision=HIGHEST)
    coarse_slabs = lax.all_to_all(coarse_back, "gx", split_axis=1, concat_axis=0, tiled=True)
    level_two = jax.nn.gelu(
        inverse_yz(coarse_slabs, half_ky, half_kz, cells_y // 2, cells_z // 2)
        + pointwise(pooled, lift_middle),
        approximate=False,
    )
    return features + pointwise(level_one + refine(level_two), project_out)


BF16 = jnp.bfloat16
MESH = pl.DeviceIdType.MESH
F32 = jnp.float32


def host_table(modes_kept, length):
    orders = np.arange(modes_kept)[:, None]
    points = np.arange(length)[None, :]
    scales = np.where(orders == 0, np.sqrt(1.0 / length), np.sqrt(2.0 / length))
    return scales * np.cos(np.pi * orders * (2 * points + 1) / (2 * length))


def host_split(table):
    table = np.asarray(table, np.float32)
    high = table.astype(jnp.bfloat16)
    low = (table - high.astype(np.float32)).astype(jnp.bfloat16)
    return high, low


def left_rows(table):
    high, low = host_split(table)
    return jnp.asarray(
        np.concatenate([np.concatenate([high, high], 1), np.concatenate([low, low], 1)], 0)
    )


def left_three(table):
    high, low = host_split(table)
    return jnp.asarray(np.concatenate([high, high, low], 1))


def right_three(table):
    high, low = host_split(table)
    return jnp.asarray(np.concatenate([high, high, low], 0))


def split(values):
    high = values.astype(BF16)
    low = (values - high.astype(F32)).astype(BF16)
    return high, low


def dot(left, right):
    return jnp.dot(left, right, preferred_element_type=F32)


def dot_left3(left3, values):
    high, low = split(values)
    return dot(left3, jnp.concatenate([high, low, high], 0))


def dot_right3(values, right3):
    high, low = split(values)
    return dot(jnp.concatenate([high, low, high], 1), right3)


def gelu(t):
    return 0.5 * t * (1.0 + lax.erf(t * np.float32(np.sqrt(0.5))))


def far():
    return pl.BlockSpec(memory_space=pl.ANY)


def whole():
    return pl.BlockSpec(memory_space=pltpu.VMEM)


def widen(matrix_ref, targets):
    channels = matrix_ref.shape[0]
    size = channels * 8
    row = lax.broadcasted_iota(jnp.int32, (size, channels), 0) // 8
    pick = (row == lax.broadcasted_iota(jnp.int32, (size, channels), 1)).astype(F32).astype(BF16)
    col = lax.broadcasted_iota(jnp.int32, (channels, size), 1) // 8
    place = (col == lax.broadcasted_iota(jnp.int32, (channels, size), 0)).astype(F32).astype(BF16)
    left = lax.broadcasted_iota(jnp.int32, (size, size), 0) % 8
    right = lax.broadcasted_iota(jnp.int32, (size, size), 1) % 8
    for part, spots in zip(split(matrix_ref[...]), ((0, 1), (2,))):
        grown = lax.dot_general(pick, part, (((1,), (1,)), ((), ())), preferred_element_type=F32)
        grown = dot(grown.astype(BF16), place)
        for ref, at, rule in targets:
            value = jnp.where(rule(left, right), grown, 0.0).astype(BF16)
            for spot in spots:
                ref[at : at + size, spot * size : (spot + 1) * size] = value


def same(left, right):
    return left == right


def load_block(ref, at):
    channels, local_x, _, cells_z = ref.shape
    return jnp.concatenate([ref[:, x, at, :].reshape(channels * 8, cells_z) for x in range(local_x)], 1)


def store_block(ref, at, value):
    channels, local_x, _, cells_z = ref.shape
    for x in range(local_x):
        ref[:, x, at, :] = value[:, x * cells_z : (x + 1) * cells_z].reshape(channels, 8, cells_z)


def greet(n):
    me = lax.axis_index("gx")
    barrier = pltpu.get_barrier_semaphore()
    for d in range(1, n):
        pl.semaphore_signal(barrier, 1, device_id={"gx": lax.rem(me + d, n)}, device_id_type=MESH)
    pl.semaphore_wait(barrier, n - 1)


class Exchange:
    def __init__(self, n, parts, source, target, send_sem, recv_sem, own_sem):
        self.n, self.parts, self.source, self.target = n, parts, source, target
        self.send_sem, self.recv_sem, self.own_sem = send_sem, recv_sem, own_sem
        self.me = lax.axis_index("gx")

    def copy(self, part, d):
        peer = jnp.bitwise_xor(self.me, d)
        rows = pl.ds(*self.parts[part])
        return pltpu.make_async_remote_copy(
            src_ref=self.source.at[peer, rows],
            dst_ref=self.target.at[self.me, rows],
            send_sem=self.send_sem.at[part, d],
            recv_sem=self.recv_sem.at[part, d],
            device_id={"gx": peer},
            device_id_type=MESH,
        )

    def own(self, part):
        rows = pl.ds(*self.parts[part])
        return pltpu.make_async_copy(
            self.source.at[self.me, rows], self.target.at[self.me, rows], self.own_sem.at[part]
        )

    def start(self, part):
        for d in range(self.n - 1, 0, -1):
            self.copy(part, d).start()
        self.own(part).start()

    def wait(self, part):
        for d in range(1, self.n):
            self.copy(part, d).wait()
        self.own(part).wait()

    def after(self, q, action):
        for part, chunks in enumerate(self.chunks):
            last = chunks[-1] if action == self.start else chunks[0]
            pl.when(q == last)(functools.partial(action, part))


OUT = ((0,), (1, 2))
BACK = ((0,), (1,), (2,))


def chunk_exchange(n, plan, *refs):
    rows = 3 * CHUNK // 2
    parts = [(chunks[0] * rows, len(chunks) * rows) for chunks in plan]
    exchange = Exchange(n, parts, *refs)
    exchange.chunks = plan
    return exchange


CHUNK = 16
TABLES = 8


def main_kernel(n, tx, txc, *refs):
    refs = list(refs)
    f_hbm, w_hbm, wm_hbm = refs[:3]
    matrix_hbm = refs[3:6]
    table_hbm = refs[6 : 6 + TABLES]
    slab_ref, lifted_ref, base_ref, proj_wide = refs[6 + TABLES : 10 + TABLES]
    rest = refs[10 + TABLES :]
    tables = rest[:TABLES]
    (
        f_ref, w_ref, wm_ref, lev_ref, grown_ref, wire_one, got_one, wire_two, got_two,
        modal, mixed, flat_ref, modes_ref, pooled_ref, coarse_ref, stage, got_three, back_c, got_four,
        lift_wide, middle_wide, lift_ref, middle_ref, project_ref,
        send_one, recv_one, own_one, send_two, recv_two, own_two,
        send_three, recv_three, own_three, send_four, recv_four, own_four,
        f_sem, w_sem, wm_sem, table_sem, matrix_sem,
    ) = rest[TABLES:]
    ty_ref, tz_ref, tyi_ref, tzi_ref, yc_ref, zc_ref, zp_ref, perm_ref = tables
    channels, local_x, cells_y, cells_z = f_ref.shape
    modes_x, _, _, owned = w_ref.shape
    modes_y = ty_ref.shape[0] // 2
    per = modes_y // n
    chunks = channels // CHUNK
    rows = local_x * CHUNK
    half = CHUNK // 2
    quad = 4
    size_q = 3 * half

    def at_chunk(q):
        return pl.ds(pl.multiple_of(q * size_q, 8), size_q)

    me = lax.axis_index("gx")
    barrier = pltpu.get_barrier_semaphore()
    for d in range(n - 1, 0, -1):
        pl.semaphore_signal(
            barrier, 1, device_id={"gx": jnp.bitwise_xor(me, d)}, device_id_type=MESH
        )

    loads = [
        pltpu.make_async_copy(
            f_hbm.at[pl.ds(q * CHUNK, CHUNK)], f_ref.at[pl.ds(q * CHUNK, CHUNK)], f_sem.at[q]
        )
        for q in range(chunks)
    ]
    fills = [
        pltpu.make_async_copy(source, target, table_sem.at[i])
        for i, (source, target) in enumerate(zip(table_hbm, tables))
    ]
    fills += [
        pltpu.make_async_copy(source, target, matrix_sem.at[i])
        for i, (source, target) in enumerate(
            zip(matrix_hbm, (lift_ref, middle_ref, project_ref))
        )
    ]
    loads[0].start()
    fills[0].start()
    fills[1].start()
    for load in loads[1:]:
        load.start()
    for fill in fills[2:]:
        fill.start()
    fetch = pltpu.make_async_copy(w_hbm, w_ref, w_sem)
    fetch_c = pltpu.make_async_copy(wm_hbm, wm_ref, wm_sem)

    one = chunk_exchange(n, OUT, wire_one, got_one, send_one, recv_one, own_one)
    two = chunk_exchange(n, BACK, wire_two, got_two, send_two, recv_two, own_two)
    small = [(0, stage.shape[1])]
    three = Exchange(n, small, stage, got_three, send_three, recv_three, own_three)
    four = Exchange(n, small, back_c, got_four, send_four, recv_four, own_four)

    fills[0].wait()
    fills[1].wait()
    tail_lane = lax.broadcasted_iota(jnp.int32, (3 * half, 128), 1) // 32

    def forward(q, carry):
        pltpu.make_async_copy(
            f_hbm.at[pl.ds(q * CHUNK, CHUNK)], f_ref.at[pl.ds(q * CHUNK, CHUNK)], f_sem.at[q]
        ).wait()

        def channel(c, inner):
            wide = jnp.concatenate([f_ref[q * CHUNK + c, x] for x in range(local_x)], 1)
            high, low = split(wide)
            both = dot(ty_ref[...], jnp.concatenate([high, low], 0))
            both = both[:modes_y] + both[modes_y:]
            for x in range(local_x):
                grown_ref[pl.ds(x * CHUNK + c, modes_y, stride=rows), :] = both[
                    :, x * cells_z : (x + 1) * cells_z
                ]
            return inner

        lax.fori_loop(0, CHUNK, channel, 0, unroll=8)

        def owners(b, inner):
            size = quad * per * rows
            done = dot_right3(grown_ref[pl.ds(pl.multiple_of(b * size, 8), size), :], tz_ref[...])
            for k in range(quad):
                part = done[k * per * rows : (k + 1) * per * rows]
                total = jnp.concatenate(
                    [part[g * rows + 3 * half : (g + 1) * rows] for g in range(per)], 0
                )
                for g in range(per):
                    total = jnp.where(tail_lane == g, part[g * rows : g * rows + 3 * half], total)
                wire_one[b * quad + k, at_chunk(q)] = total
            return inner

        lax.fori_loop(0, n // quad, owners, 0, unroll=2)

        @pl.when(q == 0)
        def _():
            pl.semaphore_wait(barrier, n - 1)

        one.after(q, one.start)
        return carry

    lax.fori_loop(0, chunks, forward, 0)
    fetch.start()
    fetch_c.start()

    for fill in fills[2:]:
        fill.wait()
    widen(lift_ref, ((lift_wide, 0, same),))

    def lift(b, carry):
        at = pl.ds(pl.multiple_of(b * 8, 8), 8)
        store_block(lev_ref, at, dot_left3(lift_wide[...], load_block(f_ref, at)))
        return carry

    lax.fori_loop(0, cells_y // 8, lift, 0)
    mixed[...] = jnp.zeros_like(mixed)
    fetch.wait()
    fetch_c.wait()

    small_lane = lax.broadcasted_iota(jnp.int32, (half, 128), 1) // 32

    def absorb(q, carry):
        one.after(q, one.wait)
        for k in range(modes_x):
            first = sum(got_one[a, pl.ds(pl.multiple_of(q * size_q, 8), CHUNK)] * np.float32(tx[k, a, 0]) for a in range(n))
            second = sum(got_one[a, at_chunk(q)] * np.float32(tx[k, a, 1]) for a in range(n))
            extra = jnp.zeros((half, 128), F32)
            for g in range(3):
                piece = pltpu.roll(second[g * half : (g + 1) * half], 32 * (g + 1), 1)
                extra = jnp.where(small_lane == g, piece, extra)
            total = first + jnp.concatenate([second[CHUNK:], extra], 0)
            modal[k, pl.ds(pl.multiple_of(q * CHUNK, 8), CHUNK)] = total.astype(BF16).astype(F32)

        @pl.when(q < chunks - 1)
        def _():
            def mode(k, inner):
                total = mixed[k, :, :owned]
                for c in range(CHUNK):
                    at = q * CHUNK + c
                    total += modal[k, pl.ds(at, 1), :owned] * w_ref[k, at].astype(F32)
                mixed[k, :, :owned] = total
                return inner

            lax.fori_loop(0, modes_x, mode, 0, unroll=2)

        return carry

    lax.fori_loop(0, chunks, absorb, 0)

    wide_lane = lax.broadcasted_iota(jnp.int32, (3 * half, 128), 1)

    def back(h, carry):
        at = pl.ds(pl.multiple_of(h * CHUNK, CHUNK), CHUNK)

        def mode(k, inner):
            total = mixed[k, at, :owned]
            for c in range(channels - CHUNK, channels):
                total += modal[k, c : c + 1, :owned] * w_ref[k, c, at].astype(F32)
            mixed[k, at, :owned] = total
            return inner

        lax.fori_loop(0, modes_x, mode, 0, unroll=2)
        value = [mixed[k, at] for k in range(modes_x)]
        for a in range(n):
            first = sum(value[k] * np.float32(tx[k, a, 0]) for k in range(modes_x))
            second = sum(value[k] * np.float32(tx[k, a, 1]) for k in range(modes_x))
            rolled = jnp.concatenate(
                [pltpu.roll(second[half:], 96 - 32 * g, 1) for g in range(3)], 0
            )
            wire_two[a, at_chunk(h)] = jnp.where(
                wide_lane < 96, jnp.concatenate([first, second[:half]], 0), rolled
            )
        two.after(h, two.start)
        return carry

    lax.fori_loop(0, chunks, back, 0)

    widen(middle_ref, ((middle_wide, 0, same),))
    widen(project_ref, ((proj_wide, 0, same),))

    half_y = cells_y // 2
    modes_c = yc_ref.shape[0] // 2 - half_y
    parts = zc_ref.shape[1] // 128
    narrow = 128 // CHUNK
    coarse_lane = (
        lax.broadcasted_iota(jnp.int32, (modes_c, parts * 128), 1) // narrow % CHUNK
    )
    c_rows = modes_c + half_y

    def middle(h, carry):
        two.after(h, two.wait)

        values = [got_two[a, at_chunk(h)] for a in range(n)]
        done = dot_right3(jnp.concatenate(values, 0), tzi_ref[...])
        for a in range(n):
            part = done[a * size_q : (a + 1) * size_q]
            for g in range(per):
                at = (a * per + g) * rows
                grown_ref[at : at + size_q] = part[:, g * 128 : (g + 1) * 128]
                grown_ref[at + size_q : at + rows] = part[g * half : (g + 1) * half, per * 128 :]

        def level(pair, inner):
            sums = []
            for o in range(2):
                o = 2 * pair + o
                wide = jnp.concatenate(
                    [grown_ref[pl.ds(x * CHUNK + o, modes_y, stride=rows), :] for x in range(local_x)],
                    1,
                )
                done = dot_left3(tyi_ref[...], wide)
                at = h * CHUNK + o
                values = []
                for x in range(local_x):
                    value = gelu(lev_ref[at, x] + done[:, x * cells_z : (x + 1) * cells_z])
                    lev_ref[at, x] = value
                    values.append(value)
                sums.append(values[0] + values[1])
            high, low = split(jnp.concatenate(sums, 1))
            both = dot(yc_ref[...], jnp.concatenate([high, low], 0))
            both = both[:c_rows] + both[c_rows:]
            for o in range(2):
                part = both[:, o * 128 : (o + 1) * 128]
                o = 2 * pair + o
                flat_ref[h * CHUNK + o] = part[:half_y]
                modes_ref[pl.ds(pl.multiple_of(o * modes_c, 8), modes_c), :] = part[half_y:]
            return inner

        lax.fori_loop(0, CHUNK // 2, level, 0, unroll=8)

        done = dot_right3(modes_ref[...], zc_ref[...])
        total = jnp.zeros((modes_c, parts * 128), F32)
        for o in range(CHUNK):
            total = jnp.where(coarse_lane == o, done[o * modes_c : (o + 1) * modes_c], total)
        for p in range(parts):
            coarse_ref[pl.ds(h * modes_c * parts + p, modes_c, stride=parts), :] = total[
                :, p * 128 : (p + 1) * 128
            ]
        return carry

    lax.fori_loop(0, chunks, middle, 0)

    count = stage.shape[1]
    c_size = modes_c * parts
    for a in range(n):
        for h in range(chunks):
            stage[a, :, h * 128 : (h + 1) * 128] = coarse_ref[
                h * c_size + a * count : h * c_size + (a + 1) * count
            ]
    three.start(0)

    def project(b, carry):
        at = pl.ds(pl.multiple_of(b * 8, 8), 8)
        done = dot_left3(proj_wide[...], load_block(lev_ref, at))
        store_block(base_ref, at, load_block(f_ref, at) + done)
        return carry

    def pool(h, carry):
        at = pl.ds(h * CHUNK, CHUNK)
        high, low = split(flat_ref[at].reshape(CHUNK * half_y, 128))
        mean = dot(jnp.concatenate([high, low], 1), zp_ref[...])
        pooled_ref[at] = mean.reshape(CHUNK, half_y, 128)
        return carry

    lax.fori_loop(0, chunks, pool, 0)
    blocks = cells_y // 8
    lax.fori_loop(0, blocks // 2, project, 0, unroll=3)
    three.wait(0)
    modes_k = wm_ref.shape[1]
    wave = [
        sum(got_three[a] * np.float32(txc[k, a]) for a in range(n)) for k in range(modes_k)
    ]
    wave = jnp.concatenate(wave, 0).astype(BF16)
    turned = dot(wave, perm_ref[:, : wave.shape[1]])
    width = wave.shape[1]
    keep = (
        lax.broadcasted_iota(jnp.int32, (narrow, width), 1) // channels
        == lax.broadcasted_iota(jnp.int32, (narrow, width), 0)
    )
    outs = []
    for k in range(modes_k):
        for t in range(count):
            row = turned[k * count + t : k * count + t + 1]
            left = jnp.where(keep, jnp.broadcast_to(row, (narrow, width)), 0.0).astype(BF16)
            right = wm_ref[t * narrow : (t + 1) * narrow, k].reshape(narrow * channels, channels)
            outs.append(dot(left, right))
    high, low = split(jnp.concatenate(outs, 0))
    spread = perm_ref[: 2 * channels, width:]
    grown = dot(jnp.concatenate([high, low], 1), spread)
    ours = (
        lax.broadcasted_iota(jnp.int32, grown.shape, 1) % narrow
        == lax.broadcasted_iota(jnp.int32, grown.shape, 0) % narrow
    )
    grown = jnp.where(ours, grown, 0.0).reshape(modes_k * count, narrow, width).sum(1)
    for a in range(n):
        back_c[a] = sum(
            grown[k * count : (k + 1) * count] * np.float32(txc[k, a]) for k in range(modes_k)
        )
    four.start(0)

    def lift_coarse(g, carry):
        at = [pl.ds(pl.multiple_of(g * 16 + 8 * k, 8), 8) for k in range(2)]
        pooled = jnp.concatenate([pooled_ref[:, a, :].reshape(channels * 8, 128) for a in at], 1)
        done = dot_left3(middle_wide[...], pooled)
        for k in range(2):
            lifted_ref[:, at[k], :] = done[:, k * 128 : (k + 1) * 128].reshape(channels, 8, 128)
        return carry

    lax.fori_loop(0, half_y // 16, lift_coarse, 0)
    lax.fori_loop(blocks // 2, blocks, project, 0, unroll=3)
    four.wait(0)
    for a in range(n):
        for h in range(chunks):
            slab_ref[h * c_size + a * count : h * c_size + (a + 1) * count, :] = got_four[
                a, :, h * 128 : (h + 1) * 128
            ]


def main_call(n, tx, txc, features, weights, middle_weights, matrices, tables):
    channels, local_x, cells_y, cells_z = features.shape
    turned = jnp.transpose(weights, (1, 2, 3, 0))
    modes_x = turned.shape[0]
    size = channels * 8
    chunks = channels // CHUNK
    wire = (n, chunks * 3 * CHUNK // 2, 128)
    c_rows = (KY // 2) * (KZ // 2) // (128 // CHUNK)
    coarse = (n, c_rows // n, channels * 128 // CHUNK)
    wide = (size, 3 * size)

    def sems(slots):
        return [
            pltpu.SemaphoreType.DMA((slots, n)),
            pltpu.SemaphoreType.DMA((slots, n)),
            pltpu.SemaphoreType.DMA((slots,)),
        ]

    return pl.pallas_call(
        functools.partial(main_kernel, n, tx, txc),
        out_shape=(
            pltpu.VMEM((c_rows * chunks, 128), F32),
            pltpu.VMEM((channels, cells_y // 2, 128), F32),
            pltpu.VMEM(features.shape, F32),
            pltpu.VMEM(wide, BF16),
        ),
        in_specs=[far()] * (6 + TABLES),
        out_specs=(whole(),) * 4,
        scratch_shapes=[pltpu.VMEM(table.shape, table.dtype) for table in tables]
        + [
            pltpu.VMEM(features.shape, F32),
            pltpu.VMEM(turned.shape, BF16),
            pltpu.VMEM(middle_weights.shape, BF16),
            pltpu.VMEM(features.shape, F32),
            pltpu.VMEM((KY * local_x * CHUNK, cells_z), F32),
            pltpu.VMEM(wire, F32),
            pltpu.VMEM(wire, F32),
            pltpu.VMEM(wire, F32),
            pltpu.VMEM(wire, F32),
            pltpu.VMEM((modes_x, channels, 128), F32),
            pltpu.VMEM((modes_x, channels, 128), F32),
            pltpu.VMEM((channels, cells_y // 2, 128), F32),
            pltpu.VMEM((CHUNK * KY // 2, 128), F32),
            pltpu.VMEM((channels, cells_y // 2, 128), F32),
            pltpu.VMEM((c_rows * chunks, 128), F32),
            pltpu.VMEM(coarse, F32),
            pltpu.VMEM(coarse, F32),
            pltpu.VMEM(coarse, F32),
            pltpu.VMEM(coarse, F32),
            pltpu.VMEM(wide, BF16),
            pltpu.VMEM(wide, BF16),
        ]
        + [pltpu.VMEM((channels, channels), F32)] * 3
        + sems(len(OUT))
        + sems(len(BACK))
        + sems(1)
        + sems(1)
        + [
            pltpu.SemaphoreType.DMA((chunks,)),
            pltpu.SemaphoreType.DMA,
            pltpu.SemaphoreType.DMA,
            pltpu.SemaphoreType.DMA((TABLES,)),
            pltpu.SemaphoreType.DMA((3,)),
        ],
        compiler_params=pltpu.CompilerParams(
            collective_id=0, has_side_effects=True, vmem_limit_bytes=48 * 1024 * 1024
        ),
        name="main",
    )(features, turned, middle_weights, *matrices, *tables)


def final_kernel(
    slab_ref, ty_hbm, tz_hbm, lifted_ref, proj_ref, base_ref, out_hbm,
    ty_ref, tz_ref, sum_ref, spec_ref, twice_ref, load_sem, save_sem,
):
    loads = [
        pltpu.make_async_copy(source, target, load_sem.at[i])
        for i, (source, target) in enumerate(
            ((ty_hbm, ty_ref), (tz_hbm, tz_ref))
        )
    ]
    for load in loads:
        load.start()
    for load in loads:
        load.wait()
    channels, half_y, _ = lifted_ref.shape
    local_x = base_ref.shape[1]
    modes = ty_ref.shape[1] // 3
    parts = tz_ref.shape[0] // (3 * 128)
    chunks = channels // CHUNK
    c_size = modes * parts
    stacked = []
    for h in range(chunks):
        wide = jnp.concatenate(
            [slab_ref[pl.ds(h * c_size + p, modes, stride=parts), :] for p in range(parts)], 1
        )
        stacked.append(dot_left3(ty_ref[...], wide))
    grown = jnp.concatenate(stacked, 0)
    high, low = split(grown)
    left = jnp.concatenate([high, low, high], 1)
    lane = lax.broadcasted_iota(jnp.int32, left.shape, 1) // (128 // CHUNK) % (CHUNK // 2)

    pairs = CHUNK // 2
    for c in range(pairs):
        done = dot(jnp.where(lane == c, left, jnp.zeros_like(left)), tz_ref[...])
        for h in range(chunks):
            for k in range(2):
                spec_ref[h * CHUNK + k * pairs + c] = done[
                    h * half_y : (h + 1) * half_y, k * 128 : (k + 1) * 128
                ]

    saves = []
    for g in range(half_y // 16):
        at = [pl.ds(g * 16 + 8 * k, 8) for k in range(2)]
        pooled = jnp.concatenate([lifted_ref[:, a, :].reshape(channels * 8, 128) for a in at], 1)
        spectral = jnp.concatenate([spec_ref[:, a, :].reshape(channels * 8, 128) for a in at], 1)
        added = dot_left3(proj_ref[...], gelu(pooled + spectral))
        for k in range(2):
            size = channels * 8
            first = (2 * g + k) * 2 * size
            for b in range(2):
                twice_ref[pl.ds(first + b, size, stride=2), :] = added[:, k * 128 : (k + 1) * 128]
            piece = twice_ref[pl.ds(first, 2 * size), :].reshape(channels, 16, 128)
            rows = pl.ds(g * 32 + 16 * k, 16)
            for x in range(local_x):
                sum_ref[:, x, rows, :] = base_ref[:, x, rows, :] + piece
            save = pltpu.make_async_copy(
                sum_ref.at[:, :, rows, :], out_hbm.at[:, :, rows, :], save_sem.at[2 * g + k]
            )
            save.start()
            saves.append(save)
    for save in saves:
        save.wait()


def on_device(features, fine_weights, middle_weights, lift_fine, lift_middle, project_out):
    channels, local_x, cells_y, cells_z = features.shape
    n = lax.axis_size("gx")
    owned = fine_weights.shape[0]
    owned_c = middle_weights.shape[0]
    half_ky, half_kz = KY // 2, KZ // 2
    narrow = 128 // CHUNK
    fits = (
        owned == 3 * KZ
        and KZ == 32
        and KY == 3 * n
        and n % 4 == 0
        and n & (n - 1) == 0
        and owned_c % narrow == 0
        and local_x == 2
        and cells_z == 128
        and cells_y % 32 == 0
        and channels == 3 * CHUNK
    )
    if not fits:
        return general_device(
            features, fine_weights, middle_weights, lift_fine, lift_middle, project_out
        )
    modes_x = fine_weights.shape[1]
    modes_c = middle_weights.shape[1]
    tx = np.asarray(host_table(modes_x, local_x * n), np.float32).reshape(modes_x, n, local_x)
    txc = np.asarray(host_table(modes_c, n), np.float32)

    half_y, half_z = cells_y // 2, cells_z // 2
    pool_y = np.repeat(np.eye(half_y), 2, axis=1) * 0.5
    pool_z = np.repeat(np.eye(half_z), 2, axis=1) * 0.25
    ty_c = host_table(half_ky, half_y)
    tz_c = host_table(half_kz, half_z)
    parts = half_kz // narrow
    chunks = channels // CHUNK
    ty = left_rows(host_table(KY, cells_y))
    tz = right_three(np.tile(host_table(KZ, cells_z).T, (1, 4)))
    yc = left_rows(np.concatenate([pool_y, ty_c @ pool_y], 0))
    zc_full = (tz_c @ pool_z).T.reshape(cells_z, parts, 1, narrow)
    zc = right_three(np.broadcast_to(zc_full, (cells_z, parts, CHUNK, narrow)).reshape(cells_z, -1))
    zp = np.repeat(pool_z, 2, axis=0).T
    zp = np.asarray(zp, jnp.bfloat16)
    zp = jnp.asarray(np.concatenate([zp, zp], 0))
    ty_i = left_three(host_table(KY, cells_y).T)
    tz_i = right_three(np.kron(np.eye(4), host_table(KZ, cells_z)))
    width = channels * narrow
    turn = np.zeros((width, 2 * width), np.float32)
    for c in range(channels):
        for j in range(narrow):
            turn[c * narrow + j, j * channels + c] = 1.0
            turn[c, width + c * narrow + j] = 1.0
            turn[channels + c, width + c * narrow + j] = 1.0
    turn = jnp.asarray(turn.astype(jnp.bfloat16))
    slab, lifted, base, projm = main_call(
        n, tx, txc, features, fine_weights, middle_weights,
        (lift_fine, lift_middle, project_out), (ty, tz, ty_i, tz_i, yc, zc, zp, turn),
    )

    tyc_i = left_three(ty_c.T)
    grown = np.zeros((parts, 2, CHUNK // 2, narrow, 2, cells_z))
    for k in range(2):
        grown[:, k, :, :, k] = np.repeat(tz_c, 2, axis=1).reshape(parts, 1, narrow, cells_z)
    tzc_i = right_three(grown.reshape(-1, 2 * cells_z))
    return pl.pallas_call(
        final_kernel,
        out_shape=jax.ShapeDtypeStruct(features.shape, F32),
        in_specs=[whole(), far(), far(), whole(), whole(), whole()],
        out_specs=far(),
        scratch_shapes=[
            pltpu.VMEM(tyc_i.shape, tyc_i.dtype),
            pltpu.VMEM(tzc_i.shape, tzc_i.dtype),
            pltpu.VMEM(features.shape, F32),
            pltpu.VMEM((channels, half_y, 128), F32),
            pltpu.VMEM((channels * half_y * 2, 128), F32),
            pltpu.SemaphoreType.DMA((2,)),
            pltpu.SemaphoreType.DMA((half_y // 8,)),
        ],
        compiler_params=pltpu.CompilerParams(vmem_limit_bytes=24 * 1024 * 1024),
        name="final",
    )(slab, tyc_i, tzc_i, lifted, projm, base)


def solution(mesh):
    in_specs = (
        P(None, ("groups", "gx"), None, None),
        P("gx", None, None, None),
        P("gx", None, None, None),
        P(),
        P(),
        P(),
    )
    out_specs = P(None, ("groups", "gx"), None, None)
    return jax.shard_map(
        on_device, mesh=mesh, in_specs=in_specs, out_specs=out_specs, check_vma=False
    )
```
